512 devices in a mesh: cls: 128 (over y, z, core), dp: 4 (over x).
Axes of the slice: x: 4, y: 8, z: 8, core: 2. Of those that a mesh axis runs over, the one named last changes fastest.
Arguments:
- images: bfloat16 [65536, 4096], P(('cls', 'dp')), may hold values from -6 to 6
- defocus: bfloat16 [65536], P(('cls', 'dp')), may hold values from 0.5 to 2
- classes: int32 [65536, 1], P(('cls', 'dp')), may hold values from 0 to 127; in each aligned block of 128 rows (0 to 127, 128 to 255, ...) at most 2 rows name the same one
- rotations: int32 [65536], P(('cls', 'dp')), may hold values from 0 to 63
- references: bfloat16 [128, 64, 4096], P('cls'), may hold values from -6 to 6
Outputs:
- refined: bfloat16 [128, 64, 4096], P('cls', 'dp')
- misfit: float32 [65536], P(('cls', 'dp'))
The draws below stay inside these ranges and needn't reach their ends.
Inputs may be any that keep to these rules, and one draw needn't show every extreme that they name: `classes`: among the rows of one device no class is named by more than 2 particles, and in every draw some device has exactly 2 particles of one class.
All inputs are finite; a program needn't handle non-finite values.
Results may differ from the reference program's by a relative error of at most 0.008.
Values may be sent and summed in bfloat16 or wider, within the bound.
No kernel may reach another device: no remote copies, remote signals or barrier semaphores. Data moves between devices by JAX's collectives and lax.ppermute only.
A program may use at most 64 MiB of HBM per device.

```python
import math
import jax
import jax.numpy as jnp
import numpy as np
from jax import lax

SIDE = 64
ROT = 64
PART_DEV = 128
CAP = 2
CLASSES = 128
PARTICLES = 65536
N_CLS = 128
N_DP = 4


def place_ends(values, own_key, low, top_value):
    shape = values.shape
    place = [jax.random.randint(jax.random.fold_in(own_key, axis), (), 0, shape[axis]) for axis in range(len(shape))]
    values = values.at[tuple(place)].set(low)
    longest = shape.index(max(shape))
    place[longest] = (place[longest] + 1) % shape[longest]
    return values.at[tuple(place)].set(top_value)


def levels(rng, extent, pieces, smallest, largest):
    factor_of = 1.0
    for dim, shards_of in pieces:
        draws = jax.random.uniform(jax.random.fold_in(jax.random.fold_in(rng, 6), dim), (shards_of,), jnp.float32, smallest / len(pieces), largest / len(pieces))
        factor_of = factor_of * jnp.repeat(jnp.exp(draws), extent[dim] // shards_of).reshape((-1,) + (1,) * (len(extent) - 1 - dim))
    return factor_of


def assign_block(own_key, own, number, rows, amount, top, most, slope):
    sequence = jax.random.permutation(own_key, amount)
    crowded, usual = portions_of(amount, rows * top, most, slope, True), portions_of(amount, rows * top, most, slope, False)
    places = jnp.arange(amount)

    def named(tallies, rotation):
        used = int((tallies > 0).sum())
        fixed = max(1, used // 4)
        moved = fixed + (places - fixed + rotation * (used - fixed)) % max(1, amount - fixed)
        return jnp.zeros((amount,), jnp.int32).at[sequence[jnp.where(places < fixed, places, moved)]].set(jnp.asarray(tallies, jnp.int32))

    tallies = jnp.where(number % 4 == 0, named(crowded, number // 4), named(usual, number - number // 4 - 1))
    mixed = jax.random.permutation(jax.random.fold_in(own, 3), amount)
    source_of, sink = mixed[0:amount // 2 * 2:2], mixed[1:amount // 2 * 2:2]
    slack = jnp.minimum(tallies[source_of] - 1, most - tallies[sink]) // 2
    slack = jnp.where((source_of == sequence[0]) | (sink == sequence[0]) | (tallies[sink] == 0), 0, jnp.maximum(slack, 0))
    moved = jax.random.randint(jax.random.fold_in(own, 4), (amount // 2,), 0, 1 << 20) % (slack + 1)
    tallies = tallies.at[source_of].add(-moved).at[sink].add(moved)
    items = jnp.searchsorted(jnp.cumsum(tallies), jnp.arange(rows * top), side="right").astype(jnp.int32)
    listing = items.reshape(top, rows).T
    listing = listing[jax.random.permutation(jax.random.fold_in(own, 1), rows)]
    rotation = jax.random.randint(jax.random.fold_in(own, 2), (rows, 1), 0, top)
    return jnp.take_along_axis(listing, (jnp.arange(top)[None, :] + rotation) % top, axis=1)


def portions_of(count, total, bound, skew, full):
    loads = [(1 << 20) // math.isqrt(rank ** skew) + 1 for rank in range(1, count + 1)]
    largest = bound if full else min(bound, max(-(-total // count), total * loads[0] // sum(loads)))
    least = 1 if total - largest >= count - 1 else 0
    given, spare = [largest] + [least] * (count - 1), total - largest - least * (count - 1)
    while spare > 0:
        candidates = [i for i in range(1, count) if given[i] < largest] or [i for i in range(1, count) if given[i] < bound]
        mass, remaining = sum([loads[i] for i in candidates]), spare
        for i in candidates:
            extra = min(bound - given[i], max(1, remaining * loads[i] // mass), spare)
            given[i] = given[i] + extra
            spare = spare - extra
    return np.array(given)


def scatter_about(stream_key, shape, deviation, bound, cuts=(), kind=jnp.bfloat16):
    result = jax.random.normal(stream_key, shape, jnp.float32) * deviation
    if len(cuts) > 0:
        result = levels(stream_key, shape, cuts, -0.22, 0.18) * result
    return jnp.clip(result, min=-bound, max=bound).astype(kind)


def setup_inputs(seed: int = 0) -> dict:
    streams_of = jax.random.split(jax.random.key(seed), 6)
    images = scatter_about(streams_of[0], (PARTICLES, SIDE * SIDE), 1.0, 6.0, ((0, 512),))
    defocus = jnp.clip(jnp.exp(math.log(2.0) - 1.3862944 * jax.random.uniform(streams_of[1], (PARTICLES,), jnp.float32) ** levels(streams_of[1], (PARTICLES,), ((0, 512),), -0.2, 0.2)), 0.5, 2.0).astype(jnp.bfloat16)
    classes_keys = jax.random.split(jax.random.fold_in(streams_of[2], 1), PARTICLES // PART_DEV)
    classes_turns = jax.random.permutation(jax.random.fold_in(streams_of[2], 3), PARTICLES // PART_DEV)
    classes = jax.vmap(lambda own, number: assign_block(jax.random.fold_in(streams_of[2], 2), own, number, PART_DEV, CLASSES, 1, CAP, 2))(classes_keys, classes_turns).reshape((PARTICLES, 1))
    rotations = place_ends(jax.random.randint(streams_of[3], (PARTICLES,), 0, ROT), jax.random.fold_in(streams_of[3], 1), 0, ROT - 1).astype(jnp.int32)
    references = scatter_about(streams_of[4], (CLASSES, ROT, SIDE * SIDE), 1.0, 6.0, ((0, 128),))
    return {"images": images, "defocus": defocus, "classes": classes, "rotations": rotations, "references": references}


def wave_table(side_count):
    pixel_index = jnp.arange(side_count * side_count, dtype=jnp.int32)
    half_side = side_count // 2
    row_freq = (pixel_index // side_count + half_side) % side_count - half_side
    col_freq = (pixel_index % side_count + half_side) % side_count - half_side
    return (row_freq * row_freq + col_freq * col_freq).astype(jnp.float32) / float(half_side * half_side)


def contrast(defocus_rows, radius):
    phase = 20.0 * defocus_rows.astype(jnp.float32)[:, None] * radius[None, :] + 0.1
    return -jnp.sin(phase) * jnp.exp(-0.5 * radius)[None, :]


def group_gradient(table, image_rows, flat_rows, defocus_rows, radius):
    tiles = table[flat_rows].astype(jnp.float32)
    contrast_rows = contrast(defocus_rows, radius)
    residual = contrast_rows * tiles - image_rows.astype(jnp.float32)
    misfit_rows = jnp.mean(residual * residual, axis=1)
    weighted = lax.optimization_barrier((contrast_rows * residual).astype(jnp.bfloat16))
    gradient = jnp.zeros(table.shape, jnp.float32).at[flat_rows].add(weighted.astype(jnp.float32))
    rounded = lax.optimization_barrier(gradient.astype(jnp.bfloat16))
    return rounded.astype(jnp.float32), misfit_rows


def refine_step(table, damping, image_groups, flat_groups, defocus_groups, radius):
    gradient = jnp.zeros(table.shape, jnp.float32)
    misfit_list = []
    for group in range(N_DP):
        group_grad, misfit_rows = group_gradient(table, image_groups[:, group].reshape(N_CLS * PART_DEV, SIDE * SIDE), flat_groups[:, group].reshape(N_CLS * PART_DEV), defocus_groups[:, group].reshape(N_CLS * PART_DEV), radius)
        gradient = gradient + group_grad
        misfit_list.append(misfit_rows.reshape(N_CLS, PART_DEV))
    fresh = (table.astype(jnp.float32) - gradient / damping[:, None]).astype(jnp.bfloat16)
    return fresh, jnp.stack(misfit_list, axis=1)


def reference(images, defocus, classes, rotations, references):
    radius = wave_table(SIDE)
    pixel_count = SIDE * SIDE
    table = references.reshape(CLASSES * ROT, pixel_count)
    flat_index = (classes[:, 0] * ROT + rotations).astype(jnp.int32)
    counts = jnp.zeros((CLASSES * ROT,), jnp.float32).at[flat_index].add(jnp.ones((PARTICLES,), jnp.float32))
    damping = 0.5 * counts + 1.0
    image_groups = images.reshape(N_CLS, N_DP, PART_DEV, pixel_count)
    flat_groups = flat_index.reshape(N_CLS, N_DP, PART_DEV)
    defocus_groups = defocus.reshape(N_CLS, N_DP, PART_DEV)
    table_first, unused_misfit = refine_step(table, damping, image_groups, flat_groups, defocus_groups, radius)
    table_second, misfit_grid = refine_step(table_first, damping, image_groups, flat_groups, defocus_groups, radius)
    return table_second.reshape(CLASSES, ROT, pixel_count), misfit_grid.reshape(PARTICLES)
```

```python
import jax
import jax.numpy as jnp
from jax import lax
from jax.experimental import pallas as pl
from jax.experimental.pallas import tpu as pltpu
from jax.sharding import PartitionSpec as P

SIDE = 64
LANES = 128
SLOTS = 2
SINE = (
    6.283185306487567,
    -41.34170192978513,
    81.60520943195752,
    -76.70366785399285,
    41.99999017747946,
    -14.337026382067323,
)
VMEM = pl.BlockSpec(memory_space=pltpu.VMEM)
SMEM = pl.BlockSpec(memory_space=pltpu.SMEM)


def column_of(row, count):
    return jnp.broadcast_to(row, (count, row.shape[1])).T


def pack_body(class_ref, rotation_ref, defocus_ref, image_ref, out_ref, key_ref, rows_ref):
    particles = image_ref.shape[0]
    tiles = image_ref.shape[1] // LANES
    groups = out_ref.shape[0] // (particles * SLOTS) - tiles
    quarter = tiles // groups
    block = SLOTS * (quarter + 1)
    class_row = jnp.broadcast_to(class_ref[...].astype(jnp.float32), (particles, particles))
    class_column = class_row.T
    down = lax.broadcasted_iota(jnp.int32, (particles, particles), 0)
    across = lax.broadcasted_iota(jnp.int32, (particles, particles), 1)
    earlier = jnp.where((class_column == class_row) & (down < across), 1.0, 0.0)
    rank = jnp.sum(earlier, axis=0, keepdims=True)
    key_ref[...] = class_ref[...] * SLOTS + rank.astype(jnp.int32)
    rotation_row = rotation_ref[...].astype(jnp.float32) + 1.0
    defocus_row = defocus_ref[...]
    for slot in range(SLOTS):
        chosen = jnp.where((class_row == down.astype(jnp.float32)) & (rank == slot), 1.0, 0.0)
        rotation_column = jnp.sum(chosen * rotation_row, axis=1, keepdims=True) - 1.0
        defocus_column = jnp.sum(chosen * defocus_row, axis=1, keepdims=True)
        meta = jnp.where(across < LANES // 2, rotation_column, defocus_column)
        chooser = chosen.astype(jnp.bfloat16)
        for group in range(groups):
            moved = jnp.dot(
                chooser,
                image_ref[:, group * quarter * LANES : (group + 1) * quarter * LANES],
                preferred_element_type=jnp.float32,
            )
            first = group * block + slot
            for tile in range(quarter):
                rows_ref[pl.ds(first + tile * SLOTS, particles, stride=groups * block), :] = moved[
                    :, tile * LANES : (tile + 1) * LANES
                ]
            rows_ref[pl.ds(first + quarter * SLOTS, particles, stride=groups * block), :] = meta
    out_ref[...] = rows_ref[...].astype(jnp.bfloat16)


def refine_body(
    recv_ref,
    table_ref,
    phase_ref,
    decay_ref,
    out_ref,
    rows_ref,
    contrast_ref,
    sums_ref,
    pick_ref,
    pick_down_ref,
    misfit_ref,
    table_next_ref,
):
    rotations = table_ref.shape[0]
    width = table_ref.shape[1]
    quarter = width // LANES
    block = SLOTS * (quarter + 1)
    sources = recv_ref.shape[0] // block
    particles = sources * SLOTS
    groups = out_ref.shape[0]
    share = rotations // groups
    step = 128
    per_slot = sources // step
    rows_ref[...] = recv_ref[...].astype(jnp.float32)
    labels = lax.broadcasted_iota(jnp.int32, (step, LANES), 1).astype(jnp.float32)

    def meta_of(index):
        slot, chunk = index // per_slot, index % per_slot
        start = chunk * (step * block) + quarter * SLOTS + slot
        return rows_ref[pl.ds(start, step, stride=block), :]

    def mark(index, counts):
        meta = meta_of(index)
        hit = jnp.where(jnp.broadcast_to(meta[:, :1], (step, LANES)) == labels, 1.0, 0.0)
        place = pl.multiple_of(index * step, step)
        pick_ref[pl.ds(place, step), :] = hit.astype(jnp.bfloat16)
        flipped = hit.T[:rotations]
        pick_down_ref[:, pl.ds(place, step)] = flipped.astype(jnp.bfloat16)
        return counts + jnp.sum(flipped, axis=1, keepdims=True)

    counts = lax.fori_loop(
        0, particles // step, mark, jnp.zeros((rotations, 1), jnp.float32)
    )
    damping = jnp.broadcast_to(0.5 * counts + 1.0, (rotations, LANES))

    def first_pass(index, carry):
        slot, chunk = index // per_slot, index % per_slot
        place = pl.multiple_of(index * step, step)
        start = chunk * (step * block) + slot
        meta = meta_of(index)
        defocus = jnp.broadcast_to(meta[:, LANES // 2 : LANES // 2 + 1], (step, LANES))
        tiles = jnp.dot(
            pick_ref[pl.ds(place, step), :rotations],
            table_ref[...],
            preferred_element_type=jnp.float32,
        )
        for tile in range(quarter):
            image = rows_ref[pl.ds(start + tile * SLOTS, step, stride=block), :]
            turn = defocus * phase_ref[tile : tile + 1, :] + (0.1 / 6.283185307179586 + 0.25)
            turn = 0.25 - jnp.abs(turn - jnp.round(turn))
            square = turn * turn
            wave = jnp.full_like(square, SINE[-1])
            for factor in SINE[-2::-1]:
                wave = wave * square + factor
            contrast = wave * turn * decay_ref[tile : tile + 1, :]
            residual = contrast * tiles[:, tile * LANES : (tile + 1) * LANES] - image
            contrast_ref[tile, pl.ds(place, step), :] = contrast
            sums_ref[pl.ds(place, step), tile * 256 : tile * 256 + 128] = (
                contrast * residual
            ).astype(jnp.bfloat16)
            sums_ref[pl.ds(place, step), tile * 256 + 128 : tile * 256 + 256] = (
                contrast * contrast
            ).astype(jnp.bfloat16)
        return carry

    lax.fori_loop(0, particles // step, first_pass, 0)
    for tile in range(quarter):
        summed = jnp.dot(
            pick_down_ref[...],
            sums_ref[:, tile * 256 : (tile + 1) * 256],
            preferred_element_type=jnp.float32,
        )
        gradient, weight = summed[:, :LANES], summed[:, LANES:]
        lanes = slice(tile * LANES, (tile + 1) * LANES)
        table = table_ref[:, lanes].astype(jnp.float32)
        table_next = (table - gradient / damping).astype(jnp.bfloat16)
        table_next_ref[:, lanes] = table_next
        table_next = table_next.astype(jnp.float32)
        gradient = gradient - weight * (table - table_next)
        refined = (table_next - gradient / damping).astype(jnp.bfloat16)
        for group in range(groups):
            out_ref[group, :share, lanes] = refined[group * share : (group + 1) * share]

    def second_pass(index, carry):
        slot, chunk = index // per_slot, index % per_slot
        place = pl.multiple_of(index * step, step)
        start = chunk * (step * block) + slot
        tiles = jnp.dot(
            pick_ref[pl.ds(place, step), :rotations],
            table_next_ref[...],
            preferred_element_type=jnp.float32,
        )
        total = jnp.zeros((step, LANES), jnp.float32)
        for tile in range(quarter):
            image = rows_ref[pl.ds(start + tile * SLOTS, step, stride=block), :]
            residual = (
                contrast_ref[tile, pl.ds(place, step), :]
                * tiles[:, tile * LANES : (tile + 1) * LANES]
                - image
            )
            total = total + residual * residual
        misfit_ref[pl.ds(place, step), :] = total
        return carry

    lax.fori_loop(0, particles // step, second_pass, 0)
    ones = jnp.full((8, LANES), 1.0 / (groups * width), jnp.float32)
    level = lax.broadcasted_iota(jnp.int32, (8, width), 0)
    for group in range(groups):
        mine = misfit_ref[pl.ds(group, particles // groups, stride=groups), :]
        mean = lax.dot_general(
            ones,
            mine,
            (((1,), (1,)), ((), ())),
            precision=lax.Precision.HIGHEST,
            preferred_element_type=jnp.float32,
        )
        high = mean.astype(jnp.bfloat16).astype(jnp.float32)
        mean = jnp.where(level[:, : mean.shape[1]] == 0, high, mean - high)
        out_ref[group, share:, : mean.shape[1]] = mean.astype(jnp.bfloat16)
        out_ref[group, share:, mean.shape[1] :] = jnp.zeros(
            (8, width - mean.shape[1]), jnp.bfloat16
        )


def spread_body(recv_ref, out_ref):
    share = recv_ref.shape[1] - 8
    homes = out_ref.shape[0] // SLOTS
    total = jnp.sum(recv_ref[:, share:, : SLOTS * homes].astype(jnp.float32), axis=0)
    total = total[0:1] + total[1:2]
    slot = lax.broadcasted_iota(jnp.int32, out_ref.shape, 0) % SLOTS
    out_ref[...] = jnp.where(slot == 0, total[:, :homes], total[:, homes:])


def join_body(recv_ref, out_ref):
    groups, share = recv_ref.shape[0], recv_ref.shape[1] - 8
    width = recv_ref.shape[2]
    for group in range(groups):
        out_ref[:, group * width : (group + 1) * width] = recv_ref[group, :share, :]


def settle_body(own_ref, recv_ref, key_ref, out_ref):
    rows, lanes = recv_ref.shape
    lane = lax.broadcasted_iota(jnp.int32, (rows, lanes), 1)
    mine = jnp.sum(
        jnp.where(lane == own_ref[0, 0], recv_ref[...], 0.0), axis=1, keepdims=True
    )
    places = lax.broadcasted_iota(jnp.int32, (rows, key_ref.shape[1]), 0)
    out_ref[...] = jnp.sum(jnp.where(places == key_ref[...], mine, 0.0), axis=0, keepdims=True)


def shards(images, defocus, classes, rotations, references):
    count_cls = lax.axis_size("cls")
    count_dp = lax.axis_size("dp")
    particles, pixels = images.shape
    rotation_count = references.shape[1]
    share = rotation_count // count_dp
    width = pixels // count_dp
    quarter = width // LANES
    block = SLOTS * (quarter + 1)
    message_rows = count_cls * count_dp * block
    sources = count_cls * count_dp
    packed, key_row = pl.pallas_call(
        pack_body,
        out_shape=(
            jax.ShapeDtypeStruct((message_rows, LANES), jnp.bfloat16),
            jax.ShapeDtypeStruct((1, particles), jnp.int32),
        ),
        in_specs=[VMEM] * 4,
        out_specs=(VMEM, VMEM),
        scratch_shapes=[pltpu.VMEM((message_rows, LANES), jnp.float32)],
        name="pack",
    )(
        classes.reshape(1, particles),
        rotations.reshape(1, particles),
        defocus.astype(jnp.float32).reshape(1, particles),
        images,
    )
    received = lax.all_to_all(
        packed.reshape(message_rows // SLOTS, SLOTS, LANES),
        ("cls", "dp"),
        split_axis=0,
        concat_axis=0,
        tiled=True,
    ).reshape(message_rows, LANES)
    group = lax.axis_index("dp")
    pixel = (
        lax.broadcasted_iota(jnp.int32, (quarter, LANES), 0) * LANES
        + lax.broadcasted_iota(jnp.int32, (quarter, LANES), 1)
        + group * width
    )
    row_freq = (pixel // SIDE + SIDE // 2) % SIDE - SIDE // 2
    col_freq = (pixel % SIDE + SIDE // 2) % SIDE - SIDE // 2
    radius = (row_freq * row_freq + col_freq * col_freq).astype(jnp.float32) / float(
        (SIDE // 2) ** 2
    )
    phase = radius * (20.0 / 6.283185307179586)
    decay = jnp.exp(-0.5 * radius)
    table = lax.dynamic_slice_in_dim(references[0], group * width, width, 1)
    spread = pl.pallas_call(
        refine_body,
        out_shape=jax.ShapeDtypeStruct((count_dp, share + 8, width), jnp.bfloat16),
        in_specs=[VMEM] * 4,
        out_specs=VMEM,
        scratch_shapes=[
            pltpu.VMEM((message_rows, LANES), jnp.float32),
            pltpu.VMEM((quarter, sources * SLOTS, LANES), jnp.float32),
            pltpu.VMEM((sources * SLOTS, quarter * 2 * LANES), jnp.bfloat16),
            pltpu.VMEM((sources * SLOTS, LANES), jnp.bfloat16),
            pltpu.VMEM((rotation_count, sources * SLOTS), jnp.bfloat16),
            pltpu.VMEM((sources * SLOTS, LANES), jnp.float32),
            pltpu.VMEM((rotation_count, width), jnp.bfloat16),
        ],
        name="refine",
    )(received, table, phase, decay)
    turned = lax.all_to_all(spread, "dp", split_axis=0, concat_axis=0, tiled=True)
    returning = pl.pallas_call(
        spread_body,
        out_shape=jax.ShapeDtypeStruct((count_cls * SLOTS, LANES), jnp.float32),
        in_specs=[VMEM],
        out_specs=VMEM,
        name="spread",
    )(turned)
    returned = lax.all_to_all(
        returning.reshape(count_cls * SLOTS, 1, LANES),
        "cls",
        split_axis=0,
        concat_axis=0,
        tiled=True,
    ).reshape(count_cls * SLOTS, LANES)
    refined = pl.pallas_call(
        join_body,
        out_shape=jax.ShapeDtypeStruct((share, pixels), jnp.bfloat16),
        in_specs=[VMEM],
        out_specs=VMEM,
        name="join",
    )(turned)
    misfit = pl.pallas_call(
        settle_body,
        out_shape=jax.ShapeDtypeStruct((1, particles), jnp.float32),
        in_specs=[SMEM, VMEM, VMEM],
        out_specs=VMEM,
        name="settle",
    )(lax.axis_index("cls").astype(jnp.int32).reshape(1, 1), returned, key_row)
    return (refined.reshape(1, share, pixels), misfit.reshape(particles))


def solution(mesh):
    in_specs = (
        P(("cls", "dp"), None),
        P(("cls", "dp")),
        P(("cls", "dp"), None),
        P(("cls", "dp")),
        P("cls", None, None),
    )
    out_specs = (P("cls", "dp", None), P(("cls", "dp")))
    return jax.shard_map(shards, mesh=mesh, in_specs=in_specs, out_specs=out_specs, check_vma=False)
```

```python
import jax
import jax.numpy as jnp
from jax import lax
from jax.experimental import pallas as pl
from jax.experimental.pallas import tpu as pltpu
from jax.sharding import PartitionSpec as P

SIDE = 64
LANES = 128
SLOTS = 2
SINE = (
    6.283185306487567,
    -41.34170192978513,
    81.60520943195752,
    -76.70366785399285,
    41.99999017747946,
    -14.337026382067323,
)
VMEM = pl.BlockSpec(memory_space=pltpu.VMEM)
SMEM = pl.BlockSpec(memory_space=pltpu.SMEM)


def column_of(row, count):
    return jnp.broadcast_to(row, (count, row.shape[1])).T


def pack_body(class_ref, rotation_ref, defocus_ref, image_ref, out_ref, key_ref, rows_ref):
    particles = image_ref.shape[0]
    tiles = image_ref.shape[1] // LANES
    groups = out_ref.shape[0] // (particles * SLOTS) - tiles
    quarter = tiles // groups
    block = SLOTS * (quarter + 1)
    class_row = jnp.broadcast_to(class_ref[...].astype(jnp.float32), (particles, particles))
    class_column = class_row.T
    down = lax.broadcasted_iota(jnp.int32, (particles, particles), 0)
    across = lax.broadcasted_iota(jnp.int32, (particles, particles), 1)
    earlier = jnp.where((class_column == class_row) & (down < across), 1.0, 0.0)
    rank = jnp.sum(earlier, axis=0, keepdims=True)
    key_ref[...] = class_ref[...] * SLOTS + rank.astype(jnp.int32)
    rotation_row = rotation_ref[...].astype(jnp.float32) + 1.0
    defocus_row = defocus_ref[...].astype(jnp.float32)
    for slot in range(SLOTS):
        chosen = jnp.where((class_row == down.astype(jnp.float32)) & (rank == slot), 1.0, 0.0)
        rotation_column = jnp.sum(chosen * rotation_row, axis=1, keepdims=True) - 1.0
        defocus_column = jnp.sum(chosen * defocus_row, axis=1, keepdims=True)
        meta = jnp.where(across < LANES // 2, rotation_column, defocus_column)
        chooser = chosen.astype(jnp.bfloat16)
        for group in range(groups):
            moved = jnp.dot(
                chooser,
                image_ref[:, group * quarter * LANES : (group + 1) * quarter * LANES],
                preferred_element_type=jnp.float32,
            )
            first = group * block + slot
            for tile in range(quarter):
                rows_ref[pl.ds(first + tile * SLOTS, particles, stride=groups * block), :] = moved[
                    :, tile * LANES : (tile + 1) * LANES
                ]
            rows_ref[pl.ds(first + quarter * SLOTS, particles, stride=groups * block), :] = meta
    out_ref[...] = rows_ref[...].astype(jnp.bfloat16)


def refine_body(
    recv_ref,
    table_ref,
    wave_ref,
    out_ref,
    rows_ref,
    contrast_ref,
    sums_ref,
    pick_ref,
    pick_down_ref,
    misfit_ref,
    table_next_ref,
):
    rotations = table_ref.shape[0]
    width = table_ref.shape[1]
    quarter = width // LANES
    block = SLOTS * (quarter + 1)
    sources = recv_ref.shape[0] // block
    particles = sources * SLOTS
    groups = out_ref.shape[0]
    share = rotations // groups
    step = 128
    per_slot = sources // step
    rows_ref[...] = recv_ref[...].astype(jnp.float32)
    labels = lax.broadcasted_iota(jnp.int32, (step, LANES), 1).astype(jnp.float32)

    def meta_of(index):
        slot, chunk = index // per_slot, index % per_slot
        start = chunk * (step * block) + quarter * SLOTS + slot
        return rows_ref[pl.ds(start, step, stride=block), :]

    def mark(index, counts):
        meta = meta_of(index)
        hit = jnp.where(jnp.broadcast_to(meta[:, :1], (step, LANES)) == labels, 1.0, 0.0)
        place = pl.multiple_of(index * step, step)
        pick_ref[pl.ds(place, step), :] = hit.astype(jnp.bfloat16)
        flipped = hit.T[:rotations]
        pick_down_ref[:, pl.ds(place, step)] = flipped.astype(jnp.bfloat16)
        return counts + jnp.sum(flipped, axis=1, keepdims=True)

    counts = lax.fori_loop(
        0, particles // step, mark, jnp.zeros((rotations, 1), jnp.float32)
    )
    damping = jnp.broadcast_to(0.5 * counts + 1.0, (rotations, LANES))

    lane = lax.broadcasted_iota(jnp.int32, (step, LANES), 1)
    half = jnp.where(lane < LANES // 2, 0, 1)

    def cosine(turn, decay):
        turn = 0.25 - jnp.abs(turn - jnp.round(turn))
        square = turn * turn
        wave = jnp.full_like(square, SINE[-1])
        for factor in SINE[-2::-1]:
            wave = wave * square + factor
        return wave * (turn * decay)

    def first_pass(index, carry):
        slot, chunk = index // per_slot, index % per_slot
        place = pl.multiple_of(index * step, step)
        start = chunk * (step * block) + slot
        meta = meta_of(index)
        defocus = jnp.broadcast_to(meta[:, LANES // 2 : LANES // 2 + 1], (step, LANES))
        rows = cosine(defocus * wave_ref[0:1, :] + wave_ref[1:2, :], wave_ref[2:3, :])
        turn = defocus * wave_ref[3:4, :]
        columns = cosine(turn, wave_ref[4:5, :])
        columns_shifted = cosine(turn - 0.25, wave_ref[4:5, :])
        tiles = jnp.dot(
            pick_ref[pl.ds(place, step), :rotations],
            table_ref[...],
            preferred_element_type=jnp.float32,
        )
        for tile in range(quarter):
            image = rows_ref[pl.ds(start + tile * SLOTS, step, stride=block), :]
            spot = half + 2 * tile
            contrast = (
                jnp.take_along_axis(rows, spot, axis=1) * columns
                + jnp.take_along_axis(rows, spot + 2 * quarter, axis=1) * columns_shifted
            )
            residual = contrast * tiles[:, tile * LANES : (tile + 1) * LANES] - image
            contrast_ref[tile, pl.ds(place, step), :] = contrast
            sums_ref[pl.ds(place, step), tile * 256 : tile * 256 + 128] = (
                contrast * residual
            ).astype(jnp.bfloat16)
            sums_ref[pl.ds(place, step), tile * 256 + 128 : tile * 256 + 256] = (
                contrast * contrast
            ).astype(jnp.bfloat16)
        return carry

    lax.fori_loop(0, particles // step, first_pass, 0)
    for tile in range(quarter):
        summed = jnp.dot(
            pick_down_ref[...],
            sums_ref[:, tile * 256 : (tile + 1) * 256],
            preferred_element_type=jnp.float32,
        )
        gradient, weight = summed[:, :LANES], summed[:, LANES:]
        lanes = slice(tile * LANES, (tile + 1) * LANES)
        table = table_ref[:, lanes].astype(jnp.float32)
        table_next = (table - gradient / damping).astype(jnp.bfloat16)
        table_next_ref[:, lanes] = table_next
        table_next = table_next.astype(jnp.float32)
        gradient = gradient - weight * (table - table_next)
        refined = (table_next - gradient / damping).astype(jnp.bfloat16)
        for group in range(groups):
            out_ref[group, :share, lanes] = refined[group * share : (group + 1) * share]

    def second_pass(index, carry):
        slot, chunk = index // per_slot, index % per_slot
        place = pl.multiple_of(index * step, step)
        start = chunk * (step * block) + slot
        tiles = jnp.dot(
            pick_ref[pl.ds(place, step), :rotations],
            table_next_ref[...],
            preferred_element_type=jnp.float32,
        )
        total = jnp.zeros((step, LANES), jnp.float32)
        for tile in range(quarter):
            image = rows_ref[pl.ds(start + tile * SLOTS, step, stride=block), :]
            residual = (
                contrast_ref[tile, pl.ds(place, step), :]
                * tiles[:, tile * LANES : (tile + 1) * LANES]
                - image
            )
            total = total + residual * residual
        misfit_ref[pl.ds(place, step), :] = total
        return carry

    lax.fori_loop(0, particles // step, second_pass, 0)
    ones = jnp.full((8, LANES), 1.0 / (groups * width), jnp.float32)
    level = lax.broadcasted_iota(jnp.int32, (8, width), 0)
    for group in range(groups):
        mine = misfit_ref[pl.ds(group, particles // groups, stride=groups), :]
        mean = lax.dot_general(
            ones,
            mine,
            (((1,), (1,)), ((), ())),
            precision=lax.Precision.HIGHEST,
            preferred_element_type=jnp.float32,
        )
        high = mean.astype(jnp.bfloat16).astype(jnp.float32)
        mean = jnp.where(level[:, : mean.shape[1]] == 0, high, mean - high)
        out_ref[group, share:, : mean.shape[1]] = mean.astype(jnp.bfloat16)
        out_ref[group, share:, mean.shape[1] :] = jnp.zeros(
            (8, width - mean.shape[1]), jnp.bfloat16
        )


def spread_body(recv_ref, out_ref):
    share = recv_ref.shape[1] - 8
    homes = out_ref.shape[0] // SLOTS
    total = jnp.sum(recv_ref[:, share:, : SLOTS * homes].astype(jnp.float32), axis=0)
    total = total[0:1] + total[1:2]
    slot = lax.broadcasted_iota(jnp.int32, out_ref.shape, 0) % SLOTS
    out_ref[...] = jnp.where(slot == 0, total[:, :homes], total[:, homes:])


def join_body(recv_ref, out_ref):
    groups, share = recv_ref.shape[0], recv_ref.shape[1] - 8
    width = recv_ref.shape[2]
    for group in range(groups):
        out_ref[:, group * width : (group + 1) * width] = recv_ref[group, :share, :]


def settle_body(own_ref, recv_ref, key_ref, out_ref):
    rows, lanes = recv_ref.shape
    lane = lax.broadcasted_iota(jnp.int32, (rows, lanes), 1)
    mine = jnp.sum(
        jnp.where(lane == own_ref[0, 0], recv_ref[...], 0.0), axis=1, keepdims=True
    )
    places = lax.broadcasted_iota(jnp.int32, (rows, key_ref.shape[1]), 0)
    out_ref[...] = jnp.sum(jnp.where(places == key_ref[...], mine, 0.0), axis=0, keepdims=True)


def shards(images, defocus, classes, rotations, references):
    count_cls = lax.axis_size("cls")
    count_dp = lax.axis_size("dp")
    particles, pixels = images.shape
    rotation_count = references.shape[1]
    share = rotation_count // count_dp
    width = pixels // count_dp
    quarter = width // LANES
    block = SLOTS * (quarter + 1)
    message_rows = count_cls * count_dp * block
    sources = count_cls * count_dp
    packed, key_row = pl.pallas_call(
        pack_body,
        out_shape=(
            jax.ShapeDtypeStruct((message_rows, LANES), jnp.bfloat16),
            jax.ShapeDtypeStruct((1, particles), jnp.int32),
        ),
        in_specs=[VMEM] * 4,
        out_specs=(VMEM, VMEM),
        scratch_shapes=[pltpu.VMEM((message_rows, LANES), jnp.float32)],
        name="pack",
    )(
        classes.reshape(1, particles),
        rotations.reshape(1, particles),
        defocus.reshape(1, particles),
        images,
    )
    received = lax.all_to_all(
        packed.reshape(message_rows // SLOTS, SLOTS, LANES),
        ("cls", "dp"),
        split_axis=0,
        concat_axis=0,
        tiled=True,
    ).reshape(message_rows, LANES)
    group = lax.axis_index("dp")
    lane = jnp.arange(LANES, dtype=jnp.int32)
    rows_held = width // SIDE
    row_index = lane % rows_held + group * rows_held
    row_freq = (row_index + SIDE // 2) % SIDE - SIDE // 2
    col_freq = (lane % SIDE + SIDE // 2) % SIDE - SIDE // 2
    row_radius = (row_freq * row_freq).astype(jnp.float32) / float((SIDE // 2) ** 2)
    col_radius = (col_freq * col_freq).astype(jnp.float32) / float((SIDE // 2) ** 2)
    per_turn = 20.0 / 6.283185307179586
    offset = 0.1 / 6.283185307179586 + 0.25
    blank = jnp.zeros((LANES,), jnp.float32)
    wave = jnp.stack(
        [
            row_radius * per_turn,
            offset + jnp.where(lane < rows_held, 0.0, 0.25),
            jnp.exp(-0.5 * row_radius),
            col_radius * per_turn,
            jnp.exp(-0.5 * col_radius),
            blank,
            blank,
            blank,
        ]
    )
    table = lax.dynamic_slice_in_dim(references[0], group * width, width, 1)
    spread = pl.pallas_call(
        refine_body,
        out_shape=jax.ShapeDtypeStruct((count_dp, share + 8, width), jnp.bfloat16),
        in_specs=[VMEM] * 3,
        out_specs=VMEM,
        scratch_shapes=[
            pltpu.VMEM((message_rows, LANES), jnp.float32),
            pltpu.VMEM((quarter, sources * SLOTS, LANES), jnp.float32),
            pltpu.VMEM((sources * SLOTS, quarter * 2 * LANES), jnp.bfloat16),
            pltpu.VMEM((sources * SLOTS, LANES), jnp.bfloat16),
            pltpu.VMEM((rotation_count, sources * SLOTS), jnp.bfloat16),
            pltpu.VMEM((sources * SLOTS, LANES), jnp.float32),
            pltpu.VMEM((rotation_count, width), jnp.bfloat16),
        ],
        compiler_params=pltpu.CompilerParams(vmem_limit_bytes=22 << 20),
        name="refine",
    )(received, table, wave)
    turned = lax.all_to_all(spread, "dp", split_axis=0, concat_axis=0, tiled=True)
    returning = pl.pallas_call(
        spread_body,
        out_shape=jax.ShapeDtypeStruct((count_cls * SLOTS, LANES), jnp.float32),
        in_specs=[VMEM],
        out_specs=VMEM,
        compiler_params=pltpu.CompilerParams(vmem_limit_bytes=2 << 20),
        name="spread",
    )(turned)
    returned = lax.all_to_all(
        returning.reshape(count_cls * SLOTS, 1, LANES),
        "cls",
        split_axis=0,
        concat_axis=0,
        tiled=True,
    ).reshape(count_cls * SLOTS, LANES)
    refined = pl.pallas_call(
        join_body,
        out_shape=jax.ShapeDtypeStruct((share, pixels), jnp.bfloat16),
        in_specs=[VMEM],
        out_specs=VMEM,
        compiler_params=pltpu.CompilerParams(vmem_limit_bytes=2 << 20),
        name="join",
    )(turned)
    misfit = pl.pallas_call(
        settle_body,
        out_shape=jax.ShapeDtypeStruct((1, particles), jnp.float32),
        in_specs=[SMEM, VMEM, VMEM],
        out_specs=VMEM,
        compiler_params=pltpu.CompilerParams(vmem_limit_bytes=2 << 20),
        name="settle",
    )(lax.axis_index("cls").astype(jnp.int32).reshape(1, 1), returned, key_row)
    return (refined.reshape(1, share, pixels), misfit.reshape(particles))


def solution(mesh):
    in_specs = (
        P(("cls", "dp"), None),
        P(("cls", "dp")),
        P(("cls", "dp"), None),
        P(("cls", "dp")),
        P("cls", None, None),
    )
    out_specs = (P("cls", "dp", None), P(("cls", "dp")))
    return jax.shard_map(shards, mesh=mesh, in_specs=in_specs, out_specs=out_specs, check_vma=False)
```

```python
import jax
import jax.numpy as jnp
from jax import lax
from jax.experimental import pallas as pl
from jax.experimental.pallas import tpu as pltpu
from jax.sharding import PartitionSpec as P

SIDE = 64
LANES = 128
SLOTS = 2
PARTS = 8
SINE = (
    6.283185306487567,
    -41.34170192978513,
    81.60520943195752,
    -76.70366785399285,
    41.99999017747946,
    -14.337026382067323,
)
VMEM = pl.BlockSpec(memory_space=pltpu.VMEM)
ANY = pl.BlockSpec(memory_space=pl.ANY)
SMEM = pl.BlockSpec(memory_space=pltpu.SMEM)


def column_of(row, count):
    return jnp.broadcast_to(row, (count, row.shape[1])).T


def pack_body(
    class_ref,
    rotation_ref,
    defocus_ref,
    image_hbm,
    out_hbm,
    key_ref,
    image_ref,
    rows_ref,
    out_ref,
    load_sems,
    store_sems,
):
    particles = image_ref.shape[0]
    tiles = image_ref.shape[1] // LANES
    groups = out_ref.shape[0] // (particles * SLOTS) - tiles
    quarter = tiles // groups
    width = quarter * LANES
    block = SLOTS * (quarter + 1)

    def load(group):
        columns = pl.ds(group * width, width)
        return pltpu.make_async_copy(
            image_hbm.at[:, columns], image_ref.at[:, columns], load_sems.at[group]
        )

    def store(part):
        rows = pl.ds(part * part_rows, part_rows)
        return pltpu.make_async_copy(out_ref.at[rows], out_hbm.at[rows], store_sems.at[part])

    parts = store_sems.shape[0]
    part_rows = out_ref.shape[0] // parts
    for group in range(groups):
        load(group).start()
    class_row = jnp.broadcast_to(class_ref[...].astype(jnp.float32), (particles, particles))
    class_column = class_row.T
    down = lax.broadcasted_iota(jnp.int32, (particles, particles), 0)
    across = lax.broadcasted_iota(jnp.int32, (particles, particles), 1)
    earlier = jnp.where((class_column == class_row) & (down < across), 1.0, 0.0)
    rank = jnp.sum(earlier, axis=0, keepdims=True)
    key_ref[...] = class_ref[...] * SLOTS + rank.astype(jnp.int32)
    rotation_row = rotation_ref[...].astype(jnp.float32) + 1.0
    defocus_row = defocus_ref[...].astype(jnp.float32)
    choosers = []
    for slot in range(SLOTS):
        chosen = jnp.where((class_row == down.astype(jnp.float32)) & (rank == slot), 1.0, 0.0)
        rotation_column = jnp.sum(chosen * rotation_row, axis=1, keepdims=True) - 1.0
        defocus_column = jnp.sum(chosen * defocus_row, axis=1, keepdims=True)
        meta = jnp.where(across < LANES // 2, rotation_column, defocus_column)
        for group in range(groups):
            first = group * block + slot
            rows_ref[pl.ds(first + quarter * SLOTS, particles, stride=groups * block), :] = meta
        choosers.append(chosen.astype(jnp.bfloat16))
    for group in range(groups):
        load(group).wait()
    for group in range(groups):
        for slot in range(SLOTS):
            moved = jnp.dot(
                choosers[slot],
                image_ref[:, group * width : (group + 1) * width],
                preferred_element_type=jnp.float32,
            )
            first = group * block + slot
            for tile in range(quarter):
                rows_ref[pl.ds(first + tile * SLOTS, particles, stride=groups * block), :] = moved[
                    :, tile * LANES : (tile + 1) * LANES
                ]
    for part in range(parts):
        rows = slice(part * part_rows, (part + 1) * part_rows)
        out_ref[rows] = rows_ref[rows].astype(jnp.bfloat16)
        store(part).start()
    for part in range(parts):
        store(part).wait()


def refine_body(
    recv_ref,
    table_ref,
    wave_ref,
    widen_ref,
    out_ref,
    rows_ref,
    contrast_ref,
    sums_ref,
    pick_ref,
    pick_down_ref,
    misfit_ref,
    table_next_ref,
):
    rotations = table_ref.shape[0]
    width = table_ref.shape[1]
    quarter = width // LANES
    block = SLOTS * (quarter + 1)
    sources = recv_ref.shape[0] // block
    particles = sources * SLOTS
    groups = out_ref.shape[0]
    share = rotations // groups
    homes = sources // groups
    step = 128
    per_slot = sources // step
    rows_ref[...] = recv_ref[...].astype(jnp.float32)
    lane = lax.broadcasted_iota(jnp.int32, (step, LANES), 1)
    labels = lane.astype(jnp.float32)
    held = 2 * SLOTS * quarter

    def cosine(turn, decay):
        turn = 0.25 - jnp.abs(turn - jnp.round(turn))
        square = turn * turn
        wave = jnp.full_like(square, SINE[-1])
        for factor in SINE[-2::-1]:
            wave = wave * square + factor
        return wave * (turn * decay)

    def rounded(values):
        return values.astype(jnp.bfloat16).astype(jnp.float32)

    def first_pass(index, counts):
        slot, chunk = index // per_slot, index % per_slot
        place = pl.multiple_of(index * step, step)
        start = chunk * (step * block) + slot
        meta = rows_ref[pl.ds(start + quarter * SLOTS, step, stride=block), :]
        hit = jnp.where(jnp.broadcast_to(meta[:, :1], (step, LANES)) == labels, 1.0, 0.0)
        pick = hit.astype(jnp.bfloat16)
        pick_ref[pl.ds(place, step), :] = pick
        flipped = hit.T[:rotations]
        pick_down_ref[:, pl.ds(place, step)] = flipped.astype(jnp.bfloat16)
        defocus = jnp.broadcast_to(meta[:, LANES // 2 : LANES // 2 + 1], (step, LANES))
        rows = cosine(defocus * wave_ref[0:1, :] + wave_ref[1:2, :], wave_ref[2:3, :])
        high = rounded(rows)
        middle = rounded(rows - high)
        low = rows - high - middle
        rows = jnp.where(lane < held, high, jnp.where(lane < 2 * held, middle, low))
        columns = cosine(defocus * wave_ref[3:4, :] + wave_ref[4:5, :], wave_ref[5:6, :])
        turned = pltpu.roll(columns, LANES // 2, 1)
        columns, columns_shifted = (
            jnp.where(lane < LANES // 2, columns, turned),
            jnp.where(lane < LANES // 2, turned, columns),
        )
        wide = jnp.dot(
            rows.astype(jnp.bfloat16), widen_ref[...], preferred_element_type=jnp.float32
        )
        tiles = jnp.dot(pick[:, :rotations], table_ref[...], preferred_element_type=jnp.float32)
        for tile in range(quarter):
            image = rows_ref[pl.ds(start + tile * SLOTS, step, stride=block), :]
            contrast = (
                wide[:, tile * 256 : tile * 256 + 128] * columns
                + wide[:, tile * 256 + 128 : tile * 256 + 256] * columns_shifted
            )
            residual = contrast * tiles[:, tile * LANES : (tile + 1) * LANES] - image
            contrast_ref[tile, pl.ds(place, step), :] = contrast
            sums_ref[pl.ds(place, step), tile * 256 : tile * 256 + 128] = (
                contrast * residual
            ).astype(jnp.bfloat16)
            sums_ref[pl.ds(place, step), tile * 256 + 128 : tile * 256 + 256] = (
                contrast * contrast
            ).astype(jnp.bfloat16)
        return counts + jnp.sum(flipped, axis=1, keepdims=True)

    counts = lax.fori_loop(
        0, particles // step, first_pass, jnp.zeros((rotations, 1), jnp.float32), unroll=2
    )
    damping = jnp.broadcast_to(0.5 * counts + 1.0, (rotations, LANES))
    for tile in range(quarter):
        if tile % 2 == 0:
            summed = jnp.dot(
                pick_down_ref[...],
                sums_ref[:, tile * 256 : (tile + 2) * 256],
                preferred_element_type=jnp.float32,
            )
        spot = tile % 2 * 256
        gradient = summed[:, spot : spot + LANES]
        weight = summed[:, spot + LANES : spot + 256]
        lanes = slice(tile * LANES, (tile + 1) * LANES)
        table = table_ref[:, lanes].astype(jnp.float32)
        table_next = (table - gradient / damping).astype(jnp.bfloat16)
        table_next_ref[:, lanes] = table_next
        table_next = table_next.astype(jnp.float32)
        gradient = gradient - weight * (table - table_next)
        refined = (table_next - gradient / damping).astype(jnp.bfloat16)
        for group in range(groups):
            out_ref[group, :share, lanes] = refined[group * share : (group + 1) * share]

    def second_pass(index, carry):
        slot, chunk = index // per_slot, index % per_slot
        place = pl.multiple_of(index * step, step)
        start = chunk * (step * block) + slot
        tiles = jnp.dot(
            pick_ref[pl.ds(place, step), :rotations],
            table_next_ref[...],
            preferred_element_type=jnp.float32,
        )
        total = jnp.zeros((step, LANES), jnp.float32)
        for tile in range(quarter):
            image = rows_ref[pl.ds(start + tile * SLOTS, step, stride=block), :]
            residual = (
                contrast_ref[tile, pl.ds(place, step), :]
                * tiles[:, tile * LANES : (tile + 1) * LANES]
                - image
            )
            total = total + residual * residual
        misfit_ref[pl.ds(place, step), :] = total
        return carry

    lax.fori_loop(0, particles // step, second_pass, 0, unroll=2)
    ones = jnp.full((8, LANES), 1.0 / (groups * width), jnp.float32)
    level = lax.broadcasted_iota(jnp.int32, (8, width), 0)
    for group in range(groups):
        mine = jnp.concatenate(
            [
                misfit_ref[
                    pl.ds(slot * sources + part * (sources // 2) + group, homes // 2, stride=groups),
                    :,
                ]
                for part in range(2)
                for slot in range(SLOTS)
            ],
            axis=0,
        )
        mean = lax.dot_general(
            ones,
            mine,
            (((1,), (1,)), ((), ())),
            precision=lax.Precision.HIGHEST,
            preferred_element_type=jnp.float32,
        )
        high = mean.astype(jnp.bfloat16).astype(jnp.float32)
        mean = jnp.where(level[:, : mean.shape[1]] == 0, high, mean - high)
        out_ref[group, share:, : mean.shape[1]] = mean.astype(jnp.bfloat16)
        out_ref[group, share:, mean.shape[1] :] = jnp.zeros(
            (8, width - mean.shape[1]), jnp.bfloat16
        )


def spread_body(recv_ref, out_ref):
    share = recv_ref.shape[1] - 8
    homes, lanes = out_ref.shape
    total = jnp.sum(recv_ref[:, share:, : 2 * lanes].astype(jnp.float32), axis=0)
    total = total[0:1] + total[1:2]
    home = lax.broadcasted_iota(jnp.int32, out_ref.shape, 0)
    out_ref[...] = jnp.where(home < homes // 2, total[:, :lanes], total[:, lanes:])


def join_body(recv_ref, out_ref):
    groups, share = recv_ref.shape[0], recv_ref.shape[1] - 8
    width = recv_ref.shape[2]
    for group in range(groups):
        out_ref[:, group * width : (group + 1) * width] = recv_ref[group, :share, :]


def settle_body(own_ref, recv_ref, key_ref, out_ref):
    rows, lanes = recv_ref.shape
    lane = lax.broadcasted_iota(jnp.int32, (rows, lanes), 1)
    place = lax.broadcasted_iota(jnp.int32, (rows, key_ref.shape[1]), 0)
    own = lax.rem(own_ref[0, 0], rows // 2)
    total = jnp.zeros((rows, key_ref.shape[1]), jnp.float32)
    for slot in range(SLOTS):
        mine = jnp.sum(
            jnp.where(lane == own + slot * (rows // 2), recv_ref[...], 0.0),
            axis=1,
            keepdims=True,
        )
        total = total + jnp.where(place * SLOTS + slot == key_ref[...], mine, 0.0)
    out_ref[...] = jnp.sum(total, axis=0, keepdims=True)


def shards(images, defocus, classes, rotations, references):
    count_cls = lax.axis_size("cls")
    count_dp = lax.axis_size("dp")
    particles, pixels = images.shape
    rotation_count = references.shape[1]
    share = rotation_count // count_dp
    width = pixels // count_dp
    quarter = width // LANES
    block = SLOTS * (quarter + 1)
    message_rows = count_cls * count_dp * block
    sources = count_cls * count_dp
    packed, key_row = pl.pallas_call(
        pack_body,
        out_shape=(
            jax.ShapeDtypeStruct((message_rows, LANES), jnp.bfloat16),
            jax.ShapeDtypeStruct((1, particles), jnp.int32),
        ),
        in_specs=[VMEM, VMEM, VMEM, ANY],
        out_specs=(ANY, VMEM),
        scratch_shapes=[
            pltpu.VMEM((particles, pixels), jnp.bfloat16),
            pltpu.VMEM((message_rows, LANES), jnp.float32),
            pltpu.VMEM((message_rows, LANES), jnp.bfloat16),
            pltpu.SemaphoreType.DMA((count_dp,)),
            pltpu.SemaphoreType.DMA((PARTS,)),
        ],
        name="pack",
    )(
        classes.reshape(1, particles),
        rotations.reshape(1, particles),
        defocus.reshape(1, particles),
        images,
    )
    received = lax.all_to_all(
        packed.reshape(message_rows // SLOTS, SLOTS, LANES),
        ("cls", "dp"),
        split_axis=0,
        concat_axis=0,
        tiled=True,
    ).reshape(message_rows, LANES)
    group = lax.axis_index("dp")
    lane = jnp.arange(LANES, dtype=jnp.int32)
    held = width // SIDE
    row_index = lane % held + group * held
    row_freq = (row_index + SIDE // 2) % SIDE - SIDE // 2
    col_freq = (lane % SIDE + SIDE // 2) % SIDE - SIDE // 2
    row_radius = (row_freq * row_freq).astype(jnp.float32) / float((SIDE // 2) ** 2)
    col_radius = (col_freq * col_freq).astype(jnp.float32) / float((SIDE // 2) ** 2)
    per_turn = 20.0 / 6.283185307179586
    offset = 0.1 / 6.283185307179586 + 0.25
    blank = jnp.zeros((LANES,), jnp.float32)
    wave = jnp.stack(
        [
            row_radius * per_turn,
            offset + jnp.where(lane % (2 * held) < held, 0.0, 0.25),
            jnp.exp(-0.5 * row_radius),
            col_radius * per_turn,
            jnp.where(lane < SIDE, 0.0, -0.25),
            jnp.exp(-0.5 * col_radius),
            blank,
            blank,
        ]
    )
    source = lax.broadcasted_iota(jnp.int32, (LANES, 2 * width), 0)
    target = lax.broadcasted_iota(jnp.int32, (LANES, 2 * width), 1)
    wanted = target // LANES % 2 * held + target // (2 * LANES) * 2 + target % LANES // SIDE
    widen = ((source % (2 * held) == wanted) & (source < 6 * held)).astype(jnp.bfloat16)
    table = lax.dynamic_slice_in_dim(references[0], group * width, width, 1)
    spread = pl.pallas_call(
        refine_body,
        out_shape=jax.ShapeDtypeStruct((count_dp, share + 8, width), jnp.bfloat16),
        in_specs=[VMEM] * 4,
        out_specs=VMEM,
        scratch_shapes=[
            pltpu.VMEM((message_rows, LANES), jnp.float32),
            pltpu.VMEM((quarter, sources * SLOTS, LANES), jnp.float32),
            pltpu.VMEM((sources * SLOTS, quarter * 2 * LANES), jnp.bfloat16),
            pltpu.VMEM((sources * SLOTS, LANES), jnp.bfloat16),
            pltpu.VMEM((rotation_count, sources * SLOTS), jnp.bfloat16),
            pltpu.VMEM((sources * SLOTS, LANES), jnp.float32),
            pltpu.VMEM((rotation_count, width), jnp.bfloat16),
        ],
        compiler_params=pltpu.CompilerParams(vmem_limit_bytes=22 << 20),
        name="refine",
    )(received, table, wave, widen)
    turned = lax.all_to_all(spread, "dp", split_axis=0, concat_axis=0, tiled=True)
    returning = pl.pallas_call(
        spread_body,
        out_shape=jax.ShapeDtypeStruct((count_cls, LANES), jnp.float32),
        in_specs=[VMEM],
        out_specs=VMEM,
        compiler_params=pltpu.CompilerParams(vmem_limit_bytes=2 << 20),
        name="spread",
    )(turned)
    returned = lax.all_to_all(
        returning.reshape(count_cls, 1, LANES),
        "cls",
        split_axis=0,
        concat_axis=0,
        tiled=True,
    ).reshape(count_cls, LANES)
    refined = pl.pallas_call(
        join_body,
        out_shape=jax.ShapeDtypeStruct((share, pixels), jnp.bfloat16),
        in_specs=[VMEM],
        out_specs=VMEM,
        compiler_params=pltpu.CompilerParams(vmem_limit_bytes=2 << 20),
        name="join",
    )(turned)
    misfit = pl.pallas_call(
        settle_body,
        out_shape=jax.ShapeDtypeStruct((1, particles), jnp.float32),
        in_specs=[SMEM, VMEM, VMEM],
        out_specs=VMEM,
        compiler_params=pltpu.CompilerParams(vmem_limit_bytes=2 << 20),
        name="settle",
    )(lax.axis_index("cls").astype(jnp.int32).reshape(1, 1), returned, key_row)
    return (refined.reshape(1, share, pixels), misfit.reshape(particles))


def solution(mesh):
    in_specs = (
        P(("cls", "dp"), None),
        P(("cls", "dp")),
        P(("cls", "dp"), None),
        P(("cls", "dp")),
        P("cls", None, None),
    )
    out_specs = (P("cls", "dp", None), P(("cls", "dp")))
    return jax.shard_map(shards, mesh=mesh, in_specs=in_specs, out_specs=out_specs, check_vma=False)
```

```python
import jax
import jax.numpy as jnp
from jax import lax
from jax.experimental import pallas as pl
from jax.experimental.pallas import tpu as pltpu
from jax.sharding import PartitionSpec as P

SIDE = 64
LANES = 128
SLOTS = 2
PARTS = 2
SINE = (
    6.283185160099087,
    -41.341655032897165,
    81.60100414087813,
    -76.54978347470858,
    39.53671300031621,
)
VMEM = pl.BlockSpec(memory_space=pltpu.VMEM)
ANY = pl.BlockSpec(memory_space=pl.ANY)
SMEM = pl.BlockSpec(memory_space=pltpu.SMEM)


def column_of(row, count):
    return jnp.broadcast_to(row, (count, row.shape[1])).T


def pack_body(
    class_ref,
    rotation_ref,
    defocus_ref,
    image_ref,
    out_hbm,
    key_ref,
    rows_ref,
    out_ref,
    store_sems,
):
    particles = image_ref.shape[0]
    tiles = image_ref.shape[1] // LANES
    groups = out_ref.shape[0] // (particles * SLOTS) - tiles
    quarter = tiles // groups
    width = quarter * LANES
    block = SLOTS * (quarter + 1)

    def store(part):
        rows = pl.ds(part * part_rows, part_rows)
        return pltpu.make_async_copy(out_ref.at[rows], out_hbm.at[rows], store_sems.at[part])

    parts = store_sems.shape[0]
    part_rows = out_ref.shape[0] // parts
    class_row = jnp.broadcast_to(class_ref[...].astype(jnp.float32), (particles, particles))
    class_column = class_row.T
    down = lax.broadcasted_iota(jnp.int32, (particles, particles), 0)
    across = lax.broadcasted_iota(jnp.int32, (particles, particles), 1)
    earlier = jnp.where((class_column == class_row) & (down < across), 1.0, 0.0)
    rank = jnp.sum(earlier, axis=0, keepdims=True)
    key_ref[...] = class_ref[...] * SLOTS + rank.astype(jnp.int32)
    rotation_row = rotation_ref[...].astype(jnp.float32) + 1.0
    defocus_row = defocus_ref[...].astype(jnp.float32)
    choosers = []
    for slot in range(SLOTS):
        chosen = jnp.where((class_row == down.astype(jnp.float32)) & (rank == slot), 1.0, 0.0)
        rotation_column = jnp.sum(chosen * rotation_row, axis=1, keepdims=True) - 1.0
        defocus_column = jnp.sum(chosen * defocus_row, axis=1, keepdims=True)
        meta = jnp.where(across < LANES // 2, rotation_column, defocus_column)
        for group in range(groups):
            first = group * block + slot
            rows_ref[pl.ds(first + quarter * SLOTS, particles, stride=groups * block), :] = meta
        choosers.append(chosen.astype(jnp.bfloat16))
    owners = particles // parts
    for part in range(parts):
        for group in range(groups):
            for slot in range(SLOTS):
                moved = jnp.dot(
                    choosers[slot][part * owners : (part + 1) * owners],
                    image_ref[:, group * width : (group + 1) * width],
                    preferred_element_type=jnp.float32,
                )
                first = part * part_rows + group * block + slot
                for tile in range(quarter):
                    rows_ref[pl.ds(first + tile * SLOTS, owners, stride=groups * block), :] = (
                        moved[:, tile * LANES : (tile + 1) * LANES]
                    )
        rows = slice(part * part_rows, (part + 1) * part_rows)
        out_ref[rows] = rows_ref[rows].astype(jnp.bfloat16)
        store(part).start()
    for part in range(parts):
        store(part).wait()


def refine_body(
    recv_ref,
    table_ref,
    wave_ref,
    widen_ref,
    out_ref,
    rows_ref,
    contrast_ref,
    sums_ref,
    pick_ref,
    pick_down_ref,
    misfit_ref,
    table_next_ref,
):
    rotations = table_ref.shape[0]
    width = table_ref.shape[1]
    quarter = width // LANES
    block = SLOTS * (quarter + 1)
    sources = recv_ref.shape[0] // block
    particles = sources * SLOTS
    groups = out_ref.shape[0]
    share = rotations // groups
    homes = sources // groups
    step = 128
    per_slot = sources // step
    lane = lax.broadcasted_iota(jnp.int32, (step, LANES), 1)
    labels = lane.astype(jnp.float32)
    held = 2 * SLOTS * quarter

    def cosine(turn, decay):
        turn = 0.25 - jnp.abs(turn - jnp.round(turn))
        square = turn * turn
        wave = jnp.full_like(square, SINE[-1])
        for factor in SINE[-2::-1]:
            wave = wave * square + factor
        return wave * (turn * decay)

    def rounded(values):
        return values.astype(jnp.bfloat16).astype(jnp.float32)

    def first_pass(chunk, counts):
        held_rows = pl.ds(pl.multiple_of(chunk * (step * block), step), step * block)
        rows_ref[held_rows, :] = recv_ref[held_rows, :].astype(jnp.float32)
        for slot in range(SLOTS):
            counts = counts + first_slot(chunk, slot)
        return counts

    def first_slot(chunk, slot):
        place = pl.multiple_of(slot * sources + chunk * step, step)
        start = chunk * (step * block) + slot
        meta = rows_ref[pl.ds(start + quarter * SLOTS, step, stride=block), :]
        hit = jnp.where(jnp.broadcast_to(meta[:, :1], (step, LANES)) == labels, 1.0, 0.0)
        pick = hit.astype(jnp.bfloat16)
        pick_ref[pl.ds(place, step), :] = pick
        flipped = hit.T[:rotations]
        pick_down_ref[:, pl.ds(place, step)] = flipped.astype(jnp.bfloat16)
        defocus = jnp.broadcast_to(meta[:, LANES // 2 : LANES // 2 + 1], (step, LANES))
        rows = cosine(defocus * wave_ref[0:1, :] + wave_ref[1:2, :], wave_ref[2:3, :])
        high = rounded(rows)
        middle = rounded(rows - high)
        low = rows - high - middle
        rows = jnp.where(lane < held, high, jnp.where(lane < 2 * held, middle, low))
        columns = cosine(defocus * wave_ref[3:4, :] + wave_ref[4:5, :], wave_ref[5:6, :])
        turned = pltpu.roll(columns, LANES // 2, 1)
        columns, columns_shifted = (
            jnp.where(lane < LANES // 2, columns, turned),
            jnp.where(lane < LANES // 2, turned, columns),
        )
        wide = jnp.dot(
            rows.astype(jnp.bfloat16), widen_ref[...], preferred_element_type=jnp.float32
        )
        tiles = jnp.dot(pick[:, :rotations], table_ref[...], preferred_element_type=jnp.float32)
        for tile in range(quarter):
            image = rows_ref[pl.ds(start + tile * SLOTS, step, stride=block), :]
            contrast = (
                wide[:, tile * 256 : tile * 256 + 128] * columns
                + wide[:, tile * 256 + 128 : tile * 256 + 256] * columns_shifted
            )
            residual = contrast * tiles[:, tile * LANES : (tile + 1) * LANES] - image
            contrast_ref[tile, pl.ds(place, step), :] = contrast
            sums_ref[pl.ds(place, step), tile * 256 : tile * 256 + 128] = (
                contrast * residual
            ).astype(jnp.bfloat16)
            sums_ref[pl.ds(place, step), tile * 256 + 128 : tile * 256 + 256] = (
                contrast * contrast
            ).astype(jnp.bfloat16)
        return jnp.sum(flipped, axis=1, keepdims=True)

    counts = lax.fori_loop(0, per_slot, first_pass, jnp.zeros((rotations, 1), jnp.float32))
    damping = jnp.broadcast_to(0.5 * counts + 1.0, (rotations, LANES))
    for tile in range(quarter):
        if tile % 2 == 0:
            summed = jnp.dot(
                pick_down_ref[...],
                sums_ref[:, tile * 256 : (tile + 2) * 256],
                preferred_element_type=jnp.float32,
            )
        spot = tile % 2 * 256
        gradient = summed[:, spot : spot + LANES]
        weight = summed[:, spot + LANES : spot + 256]
        lanes = slice(tile * LANES, (tile + 1) * LANES)
        table = table_ref[:, lanes].astype(jnp.float32)
        table_next = (table - gradient / damping).astype(jnp.bfloat16)
        table_next_ref[:, lanes] = table_next
        table_next = table_next.astype(jnp.float32)
        gradient = gradient - weight * (table - table_next)
        refined = (table_next - gradient / damping).astype(jnp.bfloat16)
        for group in range(groups):
            out_ref[group, :share, lanes] = refined[group * share : (group + 1) * share]

    def second_pass(index, carry):
        slot, chunk = index // per_slot, index % per_slot
        place = pl.multiple_of(index * step, step)
        start = chunk * (step * block) + slot
        tiles = jnp.dot(
            pick_ref[pl.ds(place, step), :rotations],
            table_next_ref[...],
            preferred_element_type=jnp.float32,
        )
        total = jnp.zeros((step, LANES), jnp.float32)
        for tile in range(quarter):
            image = rows_ref[pl.ds(start + tile * SLOTS, step, stride=block), :]
            residual = (
                contrast_ref[tile, pl.ds(place, step), :]
                * tiles[:, tile * LANES : (tile + 1) * LANES]
                - image
            )
            total = total + residual * residual
        misfit_ref[pl.ds(place, step), :] = total
        return carry

    lax.fori_loop(0, particles // step, second_pass, 0, unroll=2)
    ones = jnp.full((8, LANES), 1.0 / (groups * width), jnp.float32)
    level = lax.broadcasted_iota(jnp.int32, (8, width), 0)
    for group in range(groups):
        mine = jnp.concatenate(
            [
                misfit_ref[
                    pl.ds(slot * sources + part * (sources // 2) + group, homes // 2, stride=groups),
                    :,
                ]
                for part in range(2)
                for slot in range(SLOTS)
            ],
            axis=0,
        )
        mean = lax.dot_general(
            ones,
            mine,
            (((1,), (1,)), ((), ())),
            precision=lax.Precision.HIGHEST,
            preferred_element_type=jnp.float32,
        )
        high = mean.astype(jnp.bfloat16).astype(jnp.float32)
        mean = jnp.where(level[:, : mean.shape[1]] == 0, high, mean - high)
        out_ref[group, share:, : mean.shape[1]] = mean.astype(jnp.bfloat16)
        out_ref[group, share:, mean.shape[1] :] = jnp.zeros(
            (8, width - mean.shape[1]), jnp.bfloat16
        )


def spread_body(recv_ref, out_ref):
    share = recv_ref.shape[1] - 8
    homes, lanes = out_ref.shape
    total = jnp.sum(recv_ref[:, share:, : 2 * lanes].astype(jnp.float32), axis=0)
    total = total[0:1] + total[1:2]
    home = lax.broadcasted_iota(jnp.int32, out_ref.shape, 0)
    out_ref[...] = jnp.where(home < homes // 2, total[:, :lanes], total[:, lanes:])


def join_body(recv_ref, out_ref):
    groups, share = recv_ref.shape[0], recv_ref.shape[1] - 8
    width = recv_ref.shape[2]
    for group in range(groups):
        out_ref[:, group * width : (group + 1) * width] = recv_ref[group, :share, :]


def settle_body(own_ref, recv_ref, key_ref, out_ref):
    rows, lanes = recv_ref.shape
    lane = lax.broadcasted_iota(jnp.int32, (rows, lanes), 1)
    place = lax.broadcasted_iota(jnp.int32, (rows, key_ref.shape[1]), 0)
    own = lax.rem(own_ref[0, 0], rows // 2)
    total = jnp.zeros((rows, key_ref.shape[1]), jnp.float32)
    for slot in range(SLOTS):
        mine = jnp.sum(
            jnp.where(lane == own + slot * (rows // 2), recv_ref[...], 0.0),
            axis=1,
            keepdims=True,
        )
        total = total + jnp.where(place * SLOTS + slot == key_ref[...], mine, 0.0)
    out_ref[...] = jnp.sum(total, axis=0, keepdims=True)


def shards(images, defocus, classes, rotations, references):
    count_cls = lax.axis_size("cls")
    count_dp = lax.axis_size("dp")
    particles, pixels = images.shape
    rotation_count = references.shape[1]
    share = rotation_count // count_dp
    width = pixels // count_dp
    quarter = width // LANES
    block = SLOTS * (quarter + 1)
    message_rows = count_cls * count_dp * block
    sources = count_cls * count_dp
    packed, key_row = pl.pallas_call(
        pack_body,
        out_shape=(
            jax.ShapeDtypeStruct((message_rows, LANES), jnp.bfloat16),
            jax.ShapeDtypeStruct((1, particles), jnp.int32),
        ),
        in_specs=[VMEM] * 4,
        out_specs=(ANY, VMEM),
        scratch_shapes=[
            pltpu.VMEM((message_rows, LANES), jnp.float32),
            pltpu.VMEM((message_rows, LANES), jnp.bfloat16),
            pltpu.SemaphoreType.DMA((PARTS,)),
        ],
        name="pack",
    )(
        classes.reshape(1, particles),
        rotations.reshape(1, particles),
        defocus.reshape(1, particles),
        images,
    )
    received = lax.all_to_all(
        packed.reshape(message_rows // SLOTS, SLOTS, LANES),
        ("cls", "dp"),
        split_axis=0,
        concat_axis=0,
        tiled=True,
    ).reshape(message_rows, LANES)
    group = lax.axis_index("dp")
    lane = jnp.arange(LANES, dtype=jnp.int32)
    held = width // SIDE
    row_index = lane % held + group * held
    row_freq = (row_index + SIDE // 2) % SIDE - SIDE // 2
    col_freq = (lane % SIDE + SIDE // 2) % SIDE - SIDE // 2
    row_radius = (row_freq * row_freq).astype(jnp.float32) / float((SIDE // 2) ** 2)
    col_radius = (col_freq * col_freq).astype(jnp.float32) / float((SIDE // 2) ** 2)
    per_turn = 20.0 / 6.283185307179586
    offset = 0.1 / 6.283185307179586 + 0.25
    blank = jnp.zeros((LANES,), jnp.float32)
    wave = jnp.stack(
        [
            row_radius * per_turn,
            offset + jnp.where(lane % (2 * held) < held, 0.0, 0.25),
            jnp.exp(-0.5 * row_radius),
            col_radius * per_turn,
            jnp.where(lane < SIDE, 0.0, -0.25),
            jnp.exp(-0.5 * col_radius),
            blank,
            blank,
        ]
    )
    source = lax.broadcasted_iota(jnp.int32, (LANES, 2 * width), 0)
    target = lax.broadcasted_iota(jnp.int32, (LANES, 2 * width), 1)
    wanted = target // LANES % 2 * held + target // (2 * LANES) * 2 + target % LANES // SIDE
    widen = ((source % (2 * held) == wanted) & (source < 6 * held)).astype(jnp.bfloat16)
    table = lax.dynamic_slice_in_dim(references[0], group * width, width, 1)
    spread = pl.pallas_call(
        refine_body,
        out_shape=jax.ShapeDtypeStruct((count_dp, share + 8, width), jnp.bfloat16),
        in_specs=[VMEM] * 4,
        out_specs=VMEM,
        scratch_shapes=[
            pltpu.VMEM((message_rows, LANES), jnp.float32),
            pltpu.VMEM((quarter, sources * SLOTS, LANES), jnp.float32),
            pltpu.VMEM((sources * SLOTS, quarter * 2 * LANES), jnp.bfloat16),
            pltpu.VMEM((sources * SLOTS, LANES), jnp.bfloat16),
            pltpu.VMEM((rotation_count, sources * SLOTS), jnp.bfloat16),
            pltpu.VMEM((sources * SLOTS, LANES), jnp.float32),
            pltpu.VMEM((rotation_count, width), jnp.bfloat16),
        ],
        compiler_params=pltpu.CompilerParams(vmem_limit_bytes=22 << 20),
        name="refine",
    )(received, table, wave, widen)
    turned = lax.all_to_all(spread, "dp", split_axis=0, concat_axis=0, tiled=True)
    returning = pl.pallas_call(
        spread_body,
        out_shape=jax.ShapeDtypeStruct((count_cls, LANES), jnp.float32),
        in_specs=[VMEM],
        out_specs=VMEM,
        compiler_params=pltpu.CompilerParams(vmem_limit_bytes=2 << 20),
        name="spread",
    )(turned)
    returned = lax.all_to_all(
        returning.reshape(count_cls, 1, LANES),
        "cls",
        split_axis=0,
        concat_axis=0,
        tiled=True,
    ).reshape(count_cls, LANES)
    refined = pl.pallas_call(
        join_body,
        out_shape=jax.ShapeDtypeStruct((share, pixels), jnp.bfloat16),
        in_specs=[VMEM],
        out_specs=VMEM,
        compiler_params=pltpu.CompilerParams(vmem_limit_bytes=2 << 20),
        name="join",
    )(turned)
    misfit = pl.pallas_call(
        settle_body,
        out_shape=jax.ShapeDtypeStruct((1, particles), jnp.float32),
        in_specs=[SMEM, VMEM, VMEM],
        out_specs=VMEM,
        compiler_params=pltpu.CompilerParams(vmem_limit_bytes=2 << 20),
        name="settle",
    )(lax.axis_index("cls").astype(jnp.int32).reshape(1, 1), returned, key_row)
    return (refined.reshape(1, share, pixels), misfit.reshape(particles))


def solution(mesh):
    in_specs = (
        P(("cls", "dp"), None),
        P(("cls", "dp")),
        P(("cls", "dp"), None),
        P(("cls", "dp")),
        P("cls", None, None),
    )
    out_specs = (P("cls", "dp", None), P(("cls", "dp")))
    return jax.shard_map(shards, mesh=mesh, in_specs=in_specs, out_specs=out_specs, check_vma=False)
```

```python
import jax
import jax.numpy as jnp
from jax import lax
from jax.experimental import pallas as pl
from jax.experimental.pallas import tpu as pltpu
from jax.sharding import PartitionSpec as P

SIDE = 64
LANES = 128
SLOTS = 2
PARTS = 2
SINE = (
    6.283185160099087,
    -41.341655032897165,
    81.60100414087813,
    -76.54978347470858,
    39.53671300031621,
)
VMEM = pl.BlockSpec(memory_space=pltpu.VMEM)
ANY = pl.BlockSpec(memory_space=pl.ANY)
SMEM = pl.BlockSpec(memory_space=pltpu.SMEM)


def column_of(row, count):
    return jnp.broadcast_to(row, (count, row.shape[1])).T


def pack_body(
    class_hbm,
    rotation_hbm,
    defocus_hbm,
    image_hbm,
    out_hbm,
    key_ref,
    class_ref,
    rotation_ref,
    defocus_ref,
    image_ref,
    rows_ref,
    out_ref,
    load_sems,
    store_sems,
):
    particles = image_ref.shape[0]
    tiles = image_ref.shape[1] // LANES
    groups = out_ref.shape[0] // (particles * SLOTS) - tiles
    quarter = tiles // groups
    width = quarter * LANES
    block = SLOTS * (quarter + 1)

    def store(part):
        rows = pl.ds(part * part_rows, part_rows)
        return pltpu.make_async_copy(out_ref.at[rows], out_hbm.at[rows], store_sems.at[part])

    sources = (class_hbm, rotation_hbm, defocus_hbm, image_hbm)
    targets = (class_ref, rotation_ref, defocus_ref, image_ref)
    loads = [
        pltpu.make_async_copy(source, target, load_sems.at[place])
        for place, (source, target) in enumerate(zip(sources, targets))
    ]
    for load in loads:
        load.start()
    parts = store_sems.shape[0]
    part_rows = out_ref.shape[0] // parts
    for load in loads[:3]:
        load.wait()
    class_row = jnp.broadcast_to(class_ref[...].astype(jnp.float32), (particles, particles))
    class_column = class_row.T
    down = lax.broadcasted_iota(jnp.int32, (particles, particles), 0)
    across = lax.broadcasted_iota(jnp.int32, (particles, particles), 1)
    earlier = jnp.where((class_column == class_row) & (down < across), 1.0, 0.0)
    rank = jnp.sum(earlier, axis=0, keepdims=True)
    key_ref[...] = class_ref[...] * SLOTS + rank.astype(jnp.int32)
    rotation_row = rotation_ref[...].astype(jnp.float32) + 1.0
    defocus_row = defocus_ref[...].astype(jnp.float32)
    choosers = []
    for slot in range(SLOTS):
        chosen = jnp.where((class_row == down.astype(jnp.float32)) & (rank == slot), 1.0, 0.0)
        rotation_column = jnp.sum(chosen * rotation_row, axis=1, keepdims=True) - 1.0
        defocus_column = jnp.sum(chosen * defocus_row, axis=1, keepdims=True)
        meta = jnp.where(across < LANES // 2, rotation_column, defocus_column)
        for group in range(groups):
            first = group * block + slot
            rows_ref[pl.ds(first + quarter * SLOTS, particles, stride=groups * block), :] = meta
        choosers.append(chosen.astype(jnp.bfloat16))
    loads[3].wait()
    owners = particles // parts
    for part in range(parts):
        for group in range(groups):
            for slot in range(SLOTS):
                moved = jnp.dot(
                    choosers[slot][part * owners : (part + 1) * owners],
                    image_ref[:, group * width : (group + 1) * width],
                    preferred_element_type=jnp.float32,
                )
                first = part * part_rows + group * block + slot
                for tile in range(quarter):
                    rows_ref[pl.ds(first + tile * SLOTS, owners, stride=groups * block), :] = (
                        moved[:, tile * LANES : (tile + 1) * LANES]
                    )
        rows = slice(part * part_rows, (part + 1) * part_rows)
        out_ref[rows] = rows_ref[rows].astype(jnp.bfloat16)
        store(part).start()
    for part in range(parts):
        store(part).wait()


def refine_body(
    recv_ref,
    table_ref,
    wave_ref,
    widen_ref,
    out_ref,
    rows_ref,
    contrast_ref,
    sums_ref,
    pick_ref,
    pick_down_ref,
    misfit_ref,
    table_next_ref,
):
    rotations, width = table_ref.shape[0], out_ref.shape[2]
    origin = lax.axis_index("dp") * width
    quarter = width // LANES
    block = SLOTS * (quarter + 1)
    sources = recv_ref.shape[0] // block
    particles = sources * SLOTS
    groups = out_ref.shape[0]
    share = rotations // groups
    homes = sources // groups
    step = 128
    per_slot = sources // step
    lane = lax.broadcasted_iota(jnp.int32, (step, LANES), 1)
    labels = lane.astype(jnp.float32)
    held = 2 * SLOTS * quarter

    def cosine(turn, decay):
        turn = 0.25 - jnp.abs(turn - jnp.round(turn))
        square = turn * turn
        wave = jnp.full_like(square, SINE[-1])
        for factor in SINE[-2::-1]:
            wave = wave * square + factor
        return wave * (turn * decay)

    def rounded(values):
        return values.astype(jnp.bfloat16).astype(jnp.float32)

    def first_pass(chunk, counts):
        held_rows = pl.ds(pl.multiple_of(chunk * (step * block), step), step * block)
        rows_ref[held_rows, :] = recv_ref[held_rows, :].astype(jnp.float32)
        for slot in range(SLOTS):
            counts = counts + first_slot(chunk, slot)
        return counts

    def first_slot(chunk, slot):
        place = pl.multiple_of(slot * sources + chunk * step, step)
        start = chunk * (step * block) + slot
        meta = rows_ref[pl.ds(start + quarter * SLOTS, step, stride=block), :]
        hit = jnp.where(jnp.broadcast_to(meta[:, :1], (step, LANES)) == labels, 1.0, 0.0)
        pick = hit.astype(jnp.bfloat16)
        pick_ref[pl.ds(place, step), :] = pick
        flipped = hit.T[:rotations]
        pick_down_ref[:, pl.ds(place, step)] = flipped.astype(jnp.bfloat16)
        defocus = jnp.broadcast_to(meta[:, LANES // 2 : LANES // 2 + 1], (step, LANES))
        rows = cosine(defocus * wave_ref[0:1, :] + wave_ref[1:2, :], wave_ref[2:3, :])
        high = rounded(rows)
        middle = rounded(rows - high)
        low = rows - high - middle
        rows = jnp.where(lane < held, high, jnp.where(lane < 2 * held, middle, low))
        columns = cosine(defocus * wave_ref[3:4, :] + wave_ref[4:5, :], wave_ref[5:6, :])
        turned = pltpu.roll(columns, LANES // 2, 1)
        columns, columns_shifted = (
            jnp.where(lane < LANES // 2, columns, turned),
            jnp.where(lane < LANES // 2, turned, columns),
        )
        wide = jnp.dot(
            rows.astype(jnp.bfloat16), widen_ref[...], preferred_element_type=jnp.float32
        )
        tiles = jnp.dot(
            pick[:, :rotations],
            table_ref[:, pl.ds(pl.multiple_of(origin, width), width)],
            preferred_element_type=jnp.float32,
        )
        for tile in range(quarter):
            image = rows_ref[pl.ds(start + tile * SLOTS, step, stride=block), :]
            contrast = (
                wide[:, tile * 256 : tile * 256 + 128] * columns
                + wide[:, tile * 256 + 128 : tile * 256 + 256] * columns_shifted
            )
            residual = contrast * tiles[:, tile * LANES : (tile + 1) * LANES] - image
            contrast_ref[tile, pl.ds(place, step), :] = contrast
            sums_ref[pl.ds(place, step), tile * 256 : tile * 256 + 128] = (
                contrast * residual
            ).astype(jnp.bfloat16)
            sums_ref[pl.ds(place, step), tile * 256 + 128 : tile * 256 + 256] = (
                contrast * contrast
            ).astype(jnp.bfloat16)
        return jnp.sum(flipped, axis=1, keepdims=True)

    counts = lax.fori_loop(0, per_slot, first_pass, jnp.zeros((rotations, 1), jnp.float32))
    damping = jnp.broadcast_to(0.5 * counts + 1.0, (rotations, LANES))
    for tile in range(quarter):
        if tile % 2 == 0:
            summed = jnp.dot(
                pick_down_ref[...],
                sums_ref[:, tile * 256 : (tile + 2) * 256],
                preferred_element_type=jnp.float32,
            )
        spot = tile % 2 * 256
        gradient = summed[:, spot : spot + LANES]
        weight = summed[:, spot + LANES : spot + 256]
        lanes = slice(tile * LANES, (tile + 1) * LANES)
        place = pl.multiple_of(origin + tile * LANES, LANES)
        table = table_ref[:, pl.ds(place, LANES)].astype(jnp.float32)
        table_next = (table - gradient / damping).astype(jnp.bfloat16)
        table_next_ref[:, lanes] = table_next
        table_next = table_next.astype(jnp.float32)
        gradient = gradient - weight * (table - table_next)
        refined = (table_next - gradient / damping).astype(jnp.bfloat16)
        for group in range(groups):
            out_ref[group, :share, lanes] = refined[group * share : (group + 1) * share]

    def second_pass(index, carry):
        slot, chunk = index // per_slot, index % per_slot
        place = pl.multiple_of(index * step, step)
        start = chunk * (step * block) + slot
        tiles = jnp.dot(
            pick_ref[pl.ds(place, step), :rotations],
            table_next_ref[...],
            preferred_element_type=jnp.float32,
        )
        total = jnp.zeros((step, LANES), jnp.float32)
        for tile in range(quarter):
            image = rows_ref[pl.ds(start + tile * SLOTS, step, stride=block), :]
            residual = (
                contrast_ref[tile, pl.ds(place, step), :]
                * tiles[:, tile * LANES : (tile + 1) * LANES]
                - image
            )
            total = total + residual * residual
        misfit_ref[pl.ds(place, step), :] = total
        return carry

    lax.fori_loop(0, particles // step, second_pass, 0, unroll=2)
    ones = jnp.full((8, LANES), 1.0 / (groups * width), jnp.float32)
    level = lax.broadcasted_iota(jnp.int32, (8, width), 0)
    for group in range(groups):
        mine = jnp.concatenate(
            [
                misfit_ref[
                    pl.ds(slot * sources + part * (sources // 2) + group, homes // 2, stride=groups),
                    :,
                ]
                for part in range(2)
                for slot in range(SLOTS)
            ],
            axis=0,
        )
        mean = lax.dot_general(
            ones,
            mine,
            (((1,), (1,)), ((), ())),
            precision=lax.Precision.HIGHEST,
            preferred_element_type=jnp.float32,
        )
        high = mean.astype(jnp.bfloat16).astype(jnp.float32)
        mean = jnp.where(level[:, : mean.shape[1]] == 0, high, mean - high)
        out_ref[group, share:, : mean.shape[1]] = mean.astype(jnp.bfloat16)
        out_ref[group, share:, mean.shape[1] :] = jnp.zeros(
            (8, width - mean.shape[1]), jnp.bfloat16
        )


def spread_body(recv_ref, out_ref):
    share = recv_ref.shape[1] - 8
    homes, lanes = out_ref.shape
    total = jnp.sum(recv_ref[:, share:, : 2 * lanes].astype(jnp.float32), axis=0)
    total = total[0:1] + total[1:2]
    home = lax.broadcasted_iota(jnp.int32, out_ref.shape, 0)
    out_ref[...] = jnp.where(home < homes // 2, total[:, :lanes], total[:, lanes:])


def join_body(recv_ref, out_ref):
    groups, share = recv_ref.shape[0], recv_ref.shape[1] - 8
    width = recv_ref.shape[2]
    for group in range(groups):
        out_ref[:, group * width : (group + 1) * width] = recv_ref[group, :share, :]


def settle_body(own_ref, recv_ref, key_ref, out_ref):
    rows, lanes = recv_ref.shape
    lane = lax.broadcasted_iota(jnp.int32, (rows, lanes), 1)
    place = lax.broadcasted_iota(jnp.int32, (rows, key_ref.shape[1]), 0)
    own = lax.rem(own_ref[0, 0], rows // 2)
    total = jnp.zeros((rows, key_ref.shape[1]), jnp.float32)
    for slot in range(SLOTS):
        mine = jnp.sum(
            jnp.where(lane == own + slot * (rows // 2), recv_ref[...], 0.0),
            axis=1,
            keepdims=True,
        )
        total = total + jnp.where(place * SLOTS + slot == key_ref[...], mine, 0.0)
    out_ref[...] = jnp.sum(total, axis=0, keepdims=True)


def shards(images, defocus, classes, rotations, references):
    count_cls = lax.axis_size("cls")
    count_dp = lax.axis_size("dp")
    particles, pixels = images.shape
    rotation_count = references.shape[1]
    share = rotation_count // count_dp
    width = pixels // count_dp
    quarter = width // LANES
    block = SLOTS * (quarter + 1)
    message_rows = count_cls * count_dp * block
    sources = count_cls * count_dp
    packed, key_row = pl.pallas_call(
        pack_body,
        out_shape=(
            jax.ShapeDtypeStruct((message_rows, LANES), jnp.bfloat16),
            jax.ShapeDtypeStruct((1, particles), jnp.int32),
        ),
        in_specs=[ANY] * 4,
        out_specs=(ANY, VMEM),
        scratch_shapes=[
            pltpu.VMEM((1, particles), jnp.int32),
            pltpu.VMEM((1, particles), jnp.int32),
            pltpu.VMEM((1, particles), jnp.bfloat16),
            pltpu.VMEM((particles, pixels), jnp.bfloat16),
            pltpu.VMEM((message_rows, LANES), jnp.float32),
            pltpu.VMEM((message_rows, LANES), jnp.bfloat16),
            pltpu.SemaphoreType.DMA((4,)),
            pltpu.SemaphoreType.DMA((PARTS,)),
        ],
        name="pack",
    )(
        classes.reshape(1, particles),
        rotations.reshape(1, particles),
        defocus.reshape(1, particles),
        images,
    )
    received = lax.all_to_all(
        packed.reshape(message_rows // SLOTS, SLOTS, LANES),
        ("cls", "dp"),
        split_axis=0,
        concat_axis=0,
        tiled=True,
    ).reshape(message_rows, LANES)
    group = lax.axis_index("dp")
    lane = jnp.arange(LANES, dtype=jnp.int32)
    held = width // SIDE
    row_index = lane % held + group * held
    row_freq = (row_index + SIDE // 2) % SIDE - SIDE // 2
    col_freq = (lane % SIDE + SIDE // 2) % SIDE - SIDE // 2
    row_radius = (row_freq * row_freq).astype(jnp.float32) / float((SIDE // 2) ** 2)
    col_radius = (col_freq * col_freq).astype(jnp.float32) / float((SIDE // 2) ** 2)
    per_turn = 20.0 / 6.283185307179586
    offset = 0.1 / 6.283185307179586 + 0.25
    blank = jnp.zeros((LANES,), jnp.float32)
    wave = jnp.stack(
        [
            row_radius * per_turn,
            offset + jnp.where(lane % (2 * held) < held, 0.0, 0.25),
            jnp.exp(-0.5 * row_radius),
            col_radius * per_turn,
            jnp.where(lane < SIDE, 0.0, -0.25),
            jnp.exp(-0.5 * col_radius),
            blank,
            blank,
        ]
    )
    source = lax.broadcasted_iota(jnp.int32, (LANES, 2 * width), 0)
    target = lax.broadcasted_iota(jnp.int32, (LANES, 2 * width), 1)
    wanted = target // LANES % 2 * held + target // (2 * LANES) * 2 + target % LANES // SIDE
    widen = ((source % (2 * held) == wanted) & (source < 6 * held)).astype(jnp.bfloat16)
    spread = pl.pallas_call(
        refine_body,
        out_shape=jax.ShapeDtypeStruct((count_dp, share + 8, width), jnp.bfloat16),
        in_specs=[VMEM] * 4,
        out_specs=VMEM,
        scratch_shapes=[
            pltpu.VMEM((message_rows, LANES), jnp.float32),
            pltpu.VMEM((quarter, sources * SLOTS, LANES), jnp.float32),
            pltpu.VMEM((sources * SLOTS, quarter * 2 * LANES), jnp.bfloat16),
            pltpu.VMEM((sources * SLOTS, LANES), jnp.bfloat16),
            pltpu.VMEM((rotation_count, sources * SLOTS), jnp.bfloat16),
            pltpu.VMEM((sources * SLOTS, LANES), jnp.float32),
            pltpu.VMEM((rotation_count, width), jnp.bfloat16),
        ],
        compiler_params=pltpu.CompilerParams(vmem_limit_bytes=22 << 20),
        name="refine",
    )(received, references[0], wave, widen)
    turned = lax.all_to_all(spread, "dp", split_axis=0, concat_axis=0, tiled=True)
    returning = pl.pallas_call(
        spread_body,
        out_shape=jax.ShapeDtypeStruct((count_cls, LANES), jnp.float32),
        in_specs=[VMEM],
        out_specs=VMEM,
        compiler_params=pltpu.CompilerParams(vmem_limit_bytes=2 << 20),
        name="spread",
    )(turned)
    returned = lax.all_to_all(
        returning.reshape(count_cls, 1, LANES),
        "cls",
        split_axis=0,
        concat_axis=0,
        tiled=True,
    ).reshape(count_cls, LANES)
    refined = pl.pallas_call(
        join_body,
        out_shape=jax.ShapeDtypeStruct((share, pixels), jnp.bfloat16),
        in_specs=[VMEM],
        out_specs=VMEM,
        compiler_params=pltpu.CompilerParams(vmem_limit_bytes=2 << 20),
        name="join",
    )(turned)
    misfit = pl.pallas_call(
        settle_body,
        out_shape=jax.ShapeDtypeStruct((1, particles), jnp.float32),
        in_specs=[SMEM, VMEM, VMEM],
        out_specs=VMEM,
        compiler_params=pltpu.CompilerParams(vmem_limit_bytes=2 << 20),
        name="settle",
    )(lax.axis_index("cls").astype(jnp.int32).reshape(1, 1), returned, key_row)
    return (refined.reshape(1, share, pixels), misfit.reshape(particles))


def solution(mesh):
    in_specs = (
        P(("cls", "dp"), None),
        P(("cls", "dp")),
        P(("cls", "dp"), None),
        P(("cls", "dp")),
        P("cls", None, None),
    )
    out_specs = (P("cls", "dp", None), P(("cls", "dp")))
    return jax.shard_map(shards, mesh=mesh, in_specs=in_specs, out_specs=out_specs, check_vma=False)
```

```python
import jax
import jax.numpy as jnp
from jax import lax
from jax.experimental import pallas as pl
from jax.experimental.pallas import tpu as pltpu
from jax.sharding import PartitionSpec as P

SIDE = 64
LANES = 128
SLOTS = 2
PARTS = 2
SINE = (
    6.283185160099087,
    -41.341655032897165,
    81.60100414087813,
    -76.54978347470858,
    39.53671300031621,
)
VMEM = pl.BlockSpec(memory_space=pltpu.VMEM)
ANY = pl.BlockSpec(memory_space=pl.ANY)
SMEM = pl.BlockSpec(memory_space=pltpu.SMEM)


def column_of(row, count):
    return jnp.broadcast_to(row, (count, row.shape[1])).T


def pack_body(
    class_hbm,
    rotation_hbm,
    defocus_hbm,
    image_hbm,
    out_hbm,
    key_ref,
    class_ref,
    rotation_ref,
    defocus_ref,
    image_ref,
    rows_ref,
    out_ref,
    load_sems,
    store_sems,
):
    particles = image_ref.shape[0]
    tiles = image_ref.shape[1] // LANES
    groups = out_ref.shape[0] // (particles * SLOTS) - tiles
    quarter = tiles // groups
    width = quarter * LANES
    block = SLOTS * (quarter + 1)

    def store(part):
        rows = pl.ds(part * part_rows, part_rows)
        return pltpu.make_async_copy(out_ref.at[rows], out_hbm.at[rows], store_sems.at[part])

    sources = (class_hbm, rotation_hbm, defocus_hbm, image_hbm)
    targets = (class_ref, rotation_ref, defocus_ref, image_ref)
    loads = [
        pltpu.make_async_copy(source, target, load_sems.at[place])
        for place, (source, target) in enumerate(zip(sources, targets))
    ]
    for load in loads:
        load.start()
    parts = store_sems.shape[0]
    part_rows = out_ref.shape[0] // parts
    for load in loads[:3]:
        load.wait()
    class_row = jnp.broadcast_to(class_ref[...].astype(jnp.float32), (particles, particles))
    class_column = class_row.T
    down = lax.broadcasted_iota(jnp.int32, (particles, particles), 0)
    across = lax.broadcasted_iota(jnp.int32, (particles, particles), 1)
    earlier = jnp.where((class_column == class_row) & (down < across), 1.0, 0.0)
    rank = jnp.sum(earlier, axis=0, keepdims=True)
    key_ref[...] = class_ref[...] * SLOTS + rank.astype(jnp.int32)
    rotation_row = rotation_ref[...].astype(jnp.float32) + 1.0
    defocus_row = defocus_ref[...].astype(jnp.float32)
    choosers = []
    for slot in range(SLOTS):
        chosen = jnp.where((class_row == down.astype(jnp.float32)) & (rank == slot), 1.0, 0.0)
        rotation_column = jnp.sum(chosen * rotation_row, axis=1, keepdims=True) - 1.0
        defocus_column = jnp.sum(chosen * defocus_row, axis=1, keepdims=True)
        meta = jnp.where(across < LANES // 2, rotation_column, defocus_column)
        for group in range(groups):
            first = group * block + slot
            rows_ref[pl.ds(first + quarter * SLOTS, particles, stride=groups * block), :] = meta
        choosers.append(chosen.astype(jnp.bfloat16))
    loads[3].wait()
    owners = particles // parts
    for part in range(parts):
        for group in range(groups):
            for slot in range(SLOTS):
                moved = jnp.dot(
                    choosers[slot][part * owners : (part + 1) * owners],
                    image_ref[:, group * width : (group + 1) * width],
                    preferred_element_type=jnp.float32,
                )
                first = part * part_rows + group * block + slot
                for tile in range(quarter):
                    rows_ref[pl.ds(first + tile * SLOTS, owners, stride=groups * block), :] = (
                        moved[:, tile * LANES : (tile + 1) * LANES]
                    )
        rows = slice(part * part_rows, (part + 1) * part_rows)
        out_ref[rows] = rows_ref[rows].astype(jnp.bfloat16)
        store(part).start()
    for part in range(parts):
        store(part).wait()


def refine_body(
    recv_ref,
    table_ref,
    wave_ref,
    widen_ref,
    out_ref,
    rows_ref,
    contrast_ref,
    sums_ref,
    pick_ref,
    pick_down_ref,
    misfit_ref,
    table_next_ref,
):
    rotations, width = table_ref.shape[0], out_ref.shape[2] - LANES
    origin = lax.axis_index("dp") * width
    quarter = width // LANES
    block = SLOTS * (quarter + 1)
    sources = recv_ref.shape[0] // block
    particles = sources * SLOTS
    groups = out_ref.shape[0]
    share = rotations // groups
    homes = sources // groups
    step = 128
    per_slot = sources // step
    lane = lax.broadcasted_iota(jnp.int32, (step, LANES), 1)
    labels = lane.astype(jnp.float32)
    held = 2 * SLOTS * quarter

    def cosine(turn, decay):
        turn = 0.25 - jnp.abs(turn - jnp.round(turn))
        square = turn * turn
        wave = jnp.full_like(square, SINE[-1])
        for factor in SINE[-2::-1]:
            wave = wave * square + factor
        return wave * (turn * decay)

    def rounded(values):
        return values.astype(jnp.bfloat16).astype(jnp.float32)

    def first_pass(chunk, counts):
        held_rows = pl.ds(pl.multiple_of(chunk * (step * block), step), step * block)
        rows_ref[held_rows, :] = recv_ref[held_rows, :].astype(jnp.float32)
        for slot in range(SLOTS):
            counts = counts + first_slot(chunk, slot)
        return counts

    def first_slot(chunk, slot):
        place = pl.multiple_of(slot * sources + chunk * step, step)
        start = chunk * (step * block) + slot
        meta = rows_ref[pl.ds(start + quarter * SLOTS, step, stride=block), :]
        hit = jnp.where(jnp.broadcast_to(meta[:, :1], (step, LANES)) == labels, 1.0, 0.0)
        pick = hit.astype(jnp.bfloat16)
        pick_ref[pl.ds(place, step), :] = pick
        flipped = hit.T[:rotations]
        pick_down_ref[:, pl.ds(place, step)] = flipped.astype(jnp.bfloat16)
        defocus = jnp.broadcast_to(meta[:, LANES // 2 : LANES // 2 + 1], (step, LANES))
        rows = cosine(defocus * wave_ref[0:1, :] + wave_ref[1:2, :], wave_ref[2:3, :])
        high = rounded(rows)
        middle = rounded(rows - high)
        low = rows - high - middle
        rows = jnp.where(lane < held, high, jnp.where(lane < 2 * held, middle, low))
        columns = cosine(defocus * wave_ref[3:4, :] + wave_ref[4:5, :], wave_ref[5:6, :])
        turned = pltpu.roll(columns, LANES // 2, 1)
        columns, columns_shifted = (
            jnp.where(lane < LANES // 2, columns, turned),
            jnp.where(lane < LANES // 2, turned, columns),
        )
        wide = jnp.dot(
            rows.astype(jnp.bfloat16), widen_ref[...], preferred_element_type=jnp.float32
        )
        tiles = jnp.dot(
            pick[:, :rotations],
            table_ref[:, pl.ds(pl.multiple_of(origin, width), width)],
            preferred_element_type=jnp.float32,
        )
        for tile in range(quarter):
            image = rows_ref[pl.ds(start + tile * SLOTS, step, stride=block), :]
            contrast = (
                wide[:, tile * 256 : tile * 256 + 128] * columns
                + wide[:, tile * 256 + 128 : tile * 256 + 256] * columns_shifted
            )
            residual = contrast * tiles[:, tile * LANES : (tile + 1) * LANES] - image
            contrast_ref[tile, pl.ds(place, step), :] = contrast
            sums_ref[pl.ds(place, step), tile * 256 : tile * 256 + 128] = (
                contrast * residual
            ).astype(jnp.bfloat16)
            sums_ref[pl.ds(place, step), tile * 256 + 128 : tile * 256 + 256] = (
                contrast * contrast
            ).astype(jnp.bfloat16)
        return jnp.sum(flipped, axis=1, keepdims=True)

    counts = lax.fori_loop(0, per_slot, first_pass, jnp.zeros((rotations, 1), jnp.float32))
    damping = jnp.broadcast_to(0.5 * counts + 1.0, (rotations, LANES))
    for tile in range(quarter):
        if tile % 2 == 0:
            summed = jnp.dot(
                pick_down_ref[...],
                sums_ref[:, tile * 256 : (tile + 2) * 256],
                preferred_element_type=jnp.float32,
            )
        spot = tile % 2 * 256
        gradient = summed[:, spot : spot + LANES]
        weight = summed[:, spot + LANES : spot + 256]
        lanes = slice(tile * LANES, (tile + 1) * LANES)
        place = pl.multiple_of(origin + tile * LANES, LANES)
        table = table_ref[:, pl.ds(place, LANES)].astype(jnp.float32)
        table_next = (table - gradient / damping).astype(jnp.bfloat16)
        table_next_ref[:, lanes] = table_next
        table_next = table_next.astype(jnp.float32)
        gradient = gradient - weight * (table - table_next)
        refined = (table_next - gradient / damping).astype(jnp.bfloat16)
        for group in range(groups):
            out_ref[group, :, lanes] = refined[group * share : (group + 1) * share]

    def second_pass(index, carry):
        slot, chunk = index // per_slot, index % per_slot
        place = pl.multiple_of(index * step, step)
        start = chunk * (step * block) + slot
        tiles = jnp.dot(
            pick_ref[pl.ds(place, step), :rotations],
            table_next_ref[...],
            preferred_element_type=jnp.float32,
        )
        total = jnp.zeros((step, LANES), jnp.float32)
        for tile in range(quarter):
            image = rows_ref[pl.ds(start + tile * SLOTS, step, stride=block), :]
            residual = (
                contrast_ref[tile, pl.ds(place, step), :]
                * tiles[:, tile * LANES : (tile + 1) * LANES]
                - image
            )
            total = total + residual * residual
        misfit_ref[pl.ds(place, step), :] = total
        return carry

    lax.fori_loop(0, particles // step, second_pass, 0, unroll=2)
    ones = jnp.ones((8, 2 * LANES), jnp.bfloat16)
    level = lax.broadcasted_iota(jnp.int32, (8, LANES), 0)
    for group in range(groups):
        mine = jnp.concatenate(
            [
                misfit_ref[
                    pl.ds(slot * sources + part * (sources // 2) + group, homes // 2, stride=groups),
                    :,
                ]
                for part in range(2)
                for slot in range(SLOTS)
            ],
            axis=0,
        )
        high = mine.astype(jnp.bfloat16)
        low = (mine - high.astype(jnp.float32)).astype(jnp.bfloat16)
        mean = lax.dot_general(
            ones,
            jnp.concatenate([high, low], axis=1),
            (((1,), (1,)), ((), ())),
            preferred_element_type=jnp.float32,
        ) * (1.0 / (groups * width))
        high = mean.astype(jnp.bfloat16).astype(jnp.float32)
        low = mean - high
        pieces = (high[:, :LANES], high[:, LANES:], low[:, :LANES], low[:, LANES:])
        rows = jnp.zeros((8, LANES), jnp.float32)
        for place, piece in enumerate(pieces):
            rows = jnp.where(level == place, piece, rows)
        out_ref[group, :8, width:] = rows.astype(jnp.bfloat16)
        out_ref[group, 8:, width:] = jnp.zeros((share - 8, LANES), jnp.bfloat16)


def spread_body(recv_ref, out_ref):
    homes, lanes = out_ref.shape
    width = recv_ref.shape[2] - lanes
    total = jnp.sum(recv_ref[:, :8, width:].astype(jnp.float32), axis=0)
    home = lax.broadcasted_iota(jnp.int32, out_ref.shape, 0)
    out_ref[...] = jnp.where(
        home < homes // 2, total[0:1] + total[2:3], total[1:2] + total[3:4]
    )


def join_body(recv_ref, out_ref):
    groups = recv_ref.shape[0]
    width = out_ref.shape[1] // groups
    for group in range(groups):
        out_ref[:, group * width : (group + 1) * width] = recv_ref[group, :, :width]


def settle_body(own_ref, recv_ref, key_ref, out_ref):
    rows, lanes = recv_ref.shape
    lane = lax.broadcasted_iota(jnp.int32, (rows, lanes), 1)
    place = lax.broadcasted_iota(jnp.int32, (rows, key_ref.shape[1]), 0)
    own = lax.rem(own_ref[0, 0], rows // 2)
    total = jnp.zeros((rows, key_ref.shape[1]), jnp.float32)
    for slot in range(SLOTS):
        mine = jnp.sum(
            jnp.where(lane == own + slot * (rows // 2), recv_ref[...], 0.0),
            axis=1,
            keepdims=True,
        )
        total = total + jnp.where(place * SLOTS + slot == key_ref[...], mine, 0.0)
    out_ref[...] = jnp.sum(total, axis=0, keepdims=True)


def shards(images, defocus, classes, rotations, references):
    count_cls = lax.axis_size("cls")
    count_dp = lax.axis_size("dp")
    particles, pixels = images.shape
    rotation_count = references.shape[1]
    share = rotation_count // count_dp
    width = pixels // count_dp
    quarter = width // LANES
    block = SLOTS * (quarter + 1)
    message_rows = count_cls * count_dp * block
    sources = count_cls * count_dp
    packed, key_row = pl.pallas_call(
        pack_body,
        out_shape=(
            jax.ShapeDtypeStruct((message_rows, LANES), jnp.bfloat16),
            jax.ShapeDtypeStruct((1, particles), jnp.int32),
        ),
        in_specs=[ANY] * 4,
        out_specs=(ANY, VMEM),
        scratch_shapes=[
            pltpu.VMEM((1, particles), jnp.int32),
            pltpu.VMEM((1, particles), jnp.int32),
            pltpu.VMEM((1, particles), jnp.bfloat16),
            pltpu.VMEM((particles, pixels), jnp.bfloat16),
            pltpu.VMEM((message_rows, LANES), jnp.float32),
            pltpu.VMEM((message_rows, LANES), jnp.bfloat16),
            pltpu.SemaphoreType.DMA((4,)),
            pltpu.SemaphoreType.DMA((PARTS,)),
        ],
        name="pack",
    )(
        classes.reshape(1, particles),
        rotations.reshape(1, particles),
        defocus.reshape(1, particles),
        images,
    )
    received = lax.all_to_all(
        packed.reshape(message_rows // SLOTS, SLOTS, LANES),
        ("cls", "dp"),
        split_axis=0,
        concat_axis=0,
        tiled=True,
    ).reshape(message_rows, LANES)
    group = lax.axis_index("dp")
    lane = jnp.arange(LANES, dtype=jnp.int32)
    held = width // SIDE
    row_index = lane % held + group * held
    row_freq = (row_index + SIDE // 2) % SIDE - SIDE // 2
    col_freq = (lane % SIDE + SIDE // 2) % SIDE - SIDE // 2
    row_radius = (row_freq * row_freq).astype(jnp.float32) / float((SIDE // 2) ** 2)
    col_radius = (col_freq * col_freq).astype(jnp.float32) / float((SIDE // 2) ** 2)
    per_turn = 20.0 / 6.283185307179586
    offset = 0.1 / 6.283185307179586 + 0.25
    blank = jnp.zeros((LANES,), jnp.float32)
    wave = jnp.stack(
        [
            row_radius * per_turn,
            offset + jnp.where(lane % (2 * held) < held, 0.0, 0.25),
            jnp.exp(-0.5 * row_radius),
            col_radius * per_turn,
            jnp.where(lane < SIDE, 0.0, -0.25),
            jnp.exp(-0.5 * col_radius),
            blank,
            blank,
        ]
    )
    source = lax.broadcasted_iota(jnp.int32, (LANES, 2 * width), 0)
    target = lax.broadcasted_iota(jnp.int32, (LANES, 2 * width), 1)
    wanted = target // LANES % 2 * held + target // (2 * LANES) * 2 + target % LANES // SIDE
    widen = ((source % (2 * held) == wanted) & (source < 6 * held)).astype(jnp.bfloat16)
    spread = pl.pallas_call(
        refine_body,
        out_shape=jax.ShapeDtypeStruct((count_dp, share, width + LANES), jnp.bfloat16),
        in_specs=[VMEM] * 4,
        out_specs=VMEM,
        scratch_shapes=[
            pltpu.VMEM((message_rows, LANES), jnp.float32),
            pltpu.VMEM((quarter, sources * SLOTS, LANES), jnp.float32),
            pltpu.VMEM((sources * SLOTS, quarter * 2 * LANES), jnp.bfloat16),
            pltpu.VMEM((sources * SLOTS, LANES), jnp.bfloat16),
            pltpu.VMEM((rotation_count, sources * SLOTS), jnp.bfloat16),
            pltpu.VMEM((sources * SLOTS, LANES), jnp.float32),
            pltpu.VMEM((rotation_count, width), jnp.bfloat16),
        ],
        compiler_params=pltpu.CompilerParams(vmem_limit_bytes=22 << 20),
        name="refine",
    )(received, references[0], wave, widen)
    turned = lax.all_to_all(spread, "dp", split_axis=0, concat_axis=0, tiled=True)
    returning = pl.pallas_call(
        spread_body,
        out_shape=jax.ShapeDtypeStruct((count_cls, LANES), jnp.float32),
        in_specs=[VMEM],
        out_specs=VMEM,
        compiler_params=pltpu.CompilerParams(vmem_limit_bytes=2 << 20),
        name="spread",
    )(turned)
    returned = lax.all_to_all(
        returning.reshape(count_cls, 1, LANES),
        "cls",
        split_axis=0,
        concat_axis=0,
        tiled=True,
    ).reshape(count_cls, LANES)
    refined = pl.pallas_call(
        join_body,
        out_shape=jax.ShapeDtypeStruct((share, pixels), jnp.bfloat16),
        in_specs=[VMEM],
        out_specs=VMEM,
        compiler_params=pltpu.CompilerParams(vmem_limit_bytes=2 << 20),
        name="join",
    )(turned)
    misfit = pl.pallas_call(
        settle_body,
        out_shape=jax.ShapeDtypeStruct((1, particles), jnp.float32),
        in_specs=[SMEM, VMEM, VMEM],
        out_specs=VMEM,
        compiler_params=pltpu.CompilerParams(vmem_limit_bytes=2 << 20),
        name="settle",
    )(lax.axis_index("cls").astype(jnp.int32).reshape(1, 1), returned, key_row)
    return (refined.reshape(1, share, pixels), misfit.reshape(particles))


def solution(mesh):
    in_specs = (
        P(("cls", "dp"), None),
        P(("cls", "dp")),
        P(("cls", "dp"), None),
        P(("cls", "dp")),
        P("cls", None, None),
    )
    out_specs = (P("cls", "dp", None), P(("cls", "dp")))
    return jax.shard_map(shards, mesh=mesh, in_specs=in_specs, out_specs=out_specs, check_vma=False)
```
